32 devices in a mesh: grp: 2 (over y), seq: 4 (over z), head: 4 (over x, core).
Axes of the slice: x: 2, y: 2, z: 4, core: 2. Of those that a mesh axis runs over, the one named last changes fastest.
Arguments:
- queries: bfloat16 [8, 512, 2048], P('grp', 'seq', 'head'), parts along dimension 0, may hold values from -6 to 6
- keys: bfloat16 [8, 512, 2, 2048], P('grp', 'seq', None, 'head'), parts along dimension 0, may hold values from -6 to 6
- values: bfloat16 [8, 512, 2, 2048], P('grp', 'seq', None, 'head'), parts along dimension 0, may hold values from -6 to 6
- log_gate: float32 [8, 16, 512], P('grp', 'head', 'seq'), parts along dimension 0, may hold values from -1 to 0
- beta: float32 [8, 2, 16, 512], P('grp', None, 'head', 'seq'), parts along dimension 0, may hold values from 0 to 1
- resets: int32 [8, 3], P('grp'), parts along dimension 0, may hold values from 0 to 511
- w_out: bfloat16 [2048, 2048], P('head'), may hold values from -0.1875 to 0.1875
Outputs:
- layer_out: float32 [8, 512, 2048], P('grp', 'seq', 'head'), parts along dimension 0
The draws below stay inside these ranges and needn't reach their ends.
There are 2 independent parts, one for each index of `grp`. The reference program is written for one: setup_inputs(seed, part) draws one part's arguments, and reference() takes and returns one part's arrays. A program takes and returns all parts, laid end to end along the dimension named above; an argument that names none is the same for every part. Nothing has to cross between parts.
All inputs are finite; a program needn't handle non-finite values.
Results may differ from the reference program's by a relative error of at most 0.0029.
Values sent between devices are 32-bit elements; how exact they have to be, the bound alone decides.
No kernel may reach another device: no remote copies, remote signals or barrier semaphores. Data moves between devices by JAX's collectives and lax.ppermute only.
A program may use at most 128 MiB of HBM per device.

```python
import jax
import jax.numpy as jnp
from jax import lax

WIDTH = 2048
HEAD_TOTAL = 16
HEAD_DIM = 128
TOK_DEV = 128
SEQUENCE_COUNT = 4
RESETS = 3
SEQUENCE_LENGTH = 512
N_HEAD = 4


def slow_heads(key):
    share = 0.5
    return jax.random.uniform(jax.random.fold_in(key, 11), (SEQUENCE_COUNT, HEAD_TOTAL)) < share


def log_uniform(key, shape, lower, upper):
    return jnp.exp(jax.random.uniform(key, shape, jnp.float32, jnp.log(lower), jnp.log(upper)))


def draw_log_gate(key, part):
    every_key = jax.random.split(jax.random.fold_in(key, 21), 5)
    slow = slow_heads(key)[:, :, None]
    fast_rate = log_uniform(every_key[0], (SEQUENCE_COUNT, HEAD_TOTAL, 1), 1.0 / 50.0, 1.0 / 30.0)
    rough = log_uniform(every_key[1], (SEQUENCE_COUNT, HEAD_TOTAL, SEQUENCE_LENGTH), 0.5, 2.0)
    block_factor = jnp.repeat(log_uniform(every_key[2], (SEQUENCE_COUNT, HEAD_TOTAL, SEQUENCE_LENGTH // TOK_DEV), 0.5, 2.0), TOK_DEV, axis=-1)
    decay_speed = jnp.where(slow, 0.3 / SEQUENCE_LENGTH, fast_rate) * rough * block_factor
    spike_factor = jax.random.uniform(every_key[3], (SEQUENCE_COUNT, HEAD_TOTAL, SEQUENCE_LENGTH)) < 1.5 / SEQUENCE_LENGTH
    decay_amount = jnp.log(jax.random.uniform(every_key[4], (SEQUENCE_COUNT, HEAD_TOTAL, SEQUENCE_LENGTH), jnp.float32, 0.55, 0.8))
    return -decay_speed + jnp.where(spike_factor, decay_amount, 0.0)


def draw_beta(key, part):
    every_key = jax.random.split(jax.random.fold_in(key, 31), 3)
    slow = slow_heads(key)[:, None, :, None]
    fast = log_uniform(every_key[0], (SEQUENCE_COUNT, 2, HEAD_TOTAL, SEQUENCE_LENGTH), 0.2, 0.7)
    block_factor = jnp.repeat(log_uniform(every_key[1], (SEQUENCE_COUNT, 2, HEAD_TOTAL, SEQUENCE_LENGTH // TOK_DEV), 0.7, 1.4), TOK_DEV, axis=-1)
    slow_value = 60.0 / SEQUENCE_LENGTH * log_uniform(every_key[2], (SEQUENCE_COUNT, 2, HEAD_TOTAL, SEQUENCE_LENGTH), 0.5, 2.0)
    return jnp.where(slow, slow_value, fast * block_factor)


def set_ends(values, key, smallest, high):
    longest = values.shape.index(max(values.shape))
    spots = []
    for shift in (0, 1):
        where = [jax.random.randint(jax.random.fold_in(key, axis), (), 0, length) for axis, length in enumerate(values.shape)]
        where[longest] = (where[longest] + shift) % values.shape[longest]
        spots.append(tuple(where))
    return values.at[spots[0]].set(smallest).at[spots[1]].set(high)


def raised(result, rng, source, target, blocks, factor):
    def block_of(dim):
        return (jnp.arange(result.shape[dim]) // (result.shape[dim] // blocks)).reshape((-1,) + (1,) * (result.ndim - 1 - dim))

    near = jax.random.permutation(rng, blocks)[block_of(target)]
    second = (block_of(target) + blocks // 2) % blocks
    return jnp.where((block_of(source) == near) | (block_of(source) == second), factor * result, result)


def block_scale(stream_key, shape, cuts, smallest, largest):
    level, own = 1.0, jax.random.fold_in(stream_key, 6)
    for position, shards_of in cuts:
        heights = jnp.exp(jax.random.uniform(jax.random.fold_in(own, position), (shards_of,), jnp.float32, smallest / len(cuts), largest / len(cuts)))
        level = level * jnp.repeat(heights, shape[position] // shards_of).reshape([-1 if axis == position else 1 for axis in range(len(shape))])
    return level


def centred(rng, extent, width, reach, cuts=(), kind=jnp.bfloat16):
    gain = block_scale(rng, extent, cuts, -0.22, 0.18) if cuts else 1.0
    entries = jax.random.normal(rng, extent, jnp.float32) * width * gain
    return jnp.minimum(jnp.maximum(entries, -reach), reach).astype(kind)


def noise_with(key, extent, deviation, most, cuts, heavy, kind=jnp.bfloat16):
    entries = deviation * jax.random.normal(key, extent, jnp.float32)
    if cuts:
        entries = entries * block_scale(key, extent, cuts, -0.22, 0.18)
    return jnp.clip(raised(entries, jax.random.fold_in(key, 3), *heavy), -most, most).astype(kind)


def setup_inputs(seed: int = 0, part: int = 0) -> dict:
    splits = jax.random.split(jax.random.key(seed), 8)
    part_keys = jax.random.split(jax.random.fold_in(splits[7], part), 8)
    return {
        "queries": centred(part_keys[0], (SEQUENCE_COUNT, SEQUENCE_LENGTH, HEAD_TOTAL * HEAD_DIM), 1.0, 6.0, ((1, 4), (2, 4))),
        "keys": centred(part_keys[1], (SEQUENCE_COUNT, SEQUENCE_LENGTH, 2, HEAD_TOTAL * HEAD_DIM), 1.0, 6.0, ((1, 4), (3, 4))),
        "values": centred(part_keys[2], (SEQUENCE_COUNT, SEQUENCE_LENGTH, 2, HEAD_TOTAL * HEAD_DIM), 1.0, 6.0, ((1, 4), (3, 4))),
        "log_gate": draw_log_gate(jax.random.fold_in(jax.random.fold_in(splits[7], part), 71), part),
        "beta": draw_beta(jax.random.fold_in(jax.random.fold_in(splits[7], part), 71), part),
        "resets": set_ends(jax.random.randint(part_keys[5], (SEQUENCE_COUNT, RESETS), 0, SEQUENCE_LENGTH), jax.random.fold_in(part_keys[5], 1), 0, SEQUENCE_LENGTH - 1).astype(jnp.int32),
        "w_out": noise_with(splits[6], (HEAD_TOTAL * HEAD_DIM, WIDTH), (HEAD_TOTAL * HEAD_DIM) ** -0.5, 0.1875, ((0, 4),), (0, 1, 4, 2.0)),
    }


highest = lax.Precision.HIGHEST
epsilon = 1e-06
block_tokens = 64

def unit_rows(matrix):
    return matrix * lax.rsqrt(lax.optimization_barrier(jnp.sum(matrix * matrix, axis=-1, keepdims=True)) + epsilon)

def block_terms(query_blk, key_blk, value_blk, gate_blk, beta_blk, doc_blk, start_doc):
    key_count = key_blk.shape[-2]
    head_size = key_blk.shape[-1]
    gate_sum = jnp.cumsum(gate_blk, axis=-1)
    key_index = jnp.arange(key_count)
    strict_lower = key_index[:, None] > key_index[None, :]
    lower_eq = key_index[:, None] >= key_index[None, :]
    same_doc = doc_blk[..., :, None] == doc_blk[..., None, :]
    linked = jnp.logical_and(lower_eq, same_doc)
    spread = gate_sum[..., :, None] - gate_sum[..., None, :]
    decays = jnp.where(linked, jnp.exp(jnp.where(linked, spread, 0.0)), 0.0)
    key_inner = jnp.einsum('...id,...jd->...ij', key_blk, key_blk, precision=highest)
    lower_part = jnp.where(strict_lower, beta_blk[..., :, None] * key_inner * decays, 0.0)
    system = lower_part + jnp.eye(key_count, dtype=jnp.float32)
    carried = jnp.exp(gate_sum) * (doc_blk == start_doc[..., None]).astype(jnp.float32)
    right_side = jnp.concatenate([(beta_blk * carried)[..., None] * key_blk, beta_blk[..., None] * value_blk], axis=-1)
    solved = jax.scipy.linalg.solve_triangular(system, right_side, lower=True, unit_diagonal=True)
    writes = solved[..., :head_size]
    fresh_values = solved[..., head_size:]
    closing = jnp.exp(gate_sum[..., -1:] - gate_sum) * (doc_blk == doc_blk[..., -1:]).astype(jnp.float32)
    keys_end = closing[..., None] * key_blk
    end_keep = carried[..., -1]
    eye_state = jnp.eye(head_size, dtype=jnp.float32)
    transit = end_keep[..., None, None] * eye_state - jnp.einsum('...kd,...ke->...de', keys_end, writes, precision=highest)
    filled = jnp.einsum('...kd,...ke->...de', keys_end, fresh_values, precision=highest)
    probes = jnp.einsum('...td,...jd->...tj', query_blk, key_blk, precision=highest) * decays[..., 1::2, :]
    reaches = carried[..., 1::2, None] * query_blk - jnp.einsum('...tj,...jd->...td', probes, writes, precision=highest)
    local_out = jnp.einsum('...tj,...jd->...td', probes, fresh_values, precision=highest)
    return (transit, filled, reaches, local_out)

def prepare(queries, keys, values, log_gate, beta, resets, offset):
    seq_count, tok_rows, packed = queries.shape
    head_count = log_gate.shape[1]
    head_size = packed // head_count
    blocks = tok_rows // block_tokens
    key_count = 2 * block_tokens
    positions = offset + jnp.arange(tok_rows, dtype=jnp.int32)
    doc_token = lax.optimization_barrier(jnp.sum((resets[:, :, None] <= positions[None, None, :]).astype(jnp.int32), axis=1))
    block_first = offset + block_tokens * jnp.arange(blocks, dtype=jnp.int32)
    doc_first = lax.optimization_barrier(jnp.sum((resets[:, :, None] < block_first[None, None, :]).astype(jnp.int32), axis=1))
    query_unit = unit_rows(queries.astype(jnp.float32).reshape(seq_count, blocks, block_tokens, head_count, head_size))
    query_unit = query_unit.transpose(0, 3, 1, 2, 4)
    key_unit = unit_rows(keys.astype(jnp.float32).reshape(seq_count, blocks, block_tokens, 2, head_count, head_size))
    key_unit = key_unit.transpose(0, 4, 1, 2, 3, 5).reshape(seq_count, head_count, blocks, key_count, head_size)
    value_blk = values.astype(jnp.float32).reshape(seq_count, blocks, block_tokens, 2, head_count, head_size)
    value_blk = value_blk.transpose(0, 4, 1, 2, 3, 5).reshape(seq_count, head_count, blocks, key_count, head_size)
    gate_tok = log_gate.reshape(seq_count, head_count, blocks, block_tokens)
    gate_pair = jnp.stack([gate_tok, jnp.zeros_like(gate_tok)], axis=-1).reshape(seq_count, head_count, blocks, key_count)
    beta_pair = beta.reshape(seq_count, 2, head_count, blocks, block_tokens).transpose(0, 2, 3, 4, 1)
    beta_pair = beta_pair.reshape(seq_count, head_count, blocks, key_count)
    doc_pair = jnp.repeat(doc_token.reshape(seq_count, blocks, block_tokens), 2, axis=-1)[:, None]
    return (query_unit, key_unit, value_blk, gate_pair, beta_pair, doc_pair, doc_first[:, None])

def reference(queries, keys, values, log_gate, beta, resets, w_out):
    seq_count, tok_rows, packed = queries.shape
    head_count = log_gate.shape[1]
    head_size = packed // head_count
    parts = prepare(queries, keys, values, log_gate, beta, resets, 0)
    moved = tuple((jnp.moveaxis(member, 2, 0) for member in parts))

    def advance(state, inputs):
        transit, filled, reaches, local_out = block_terms(*inputs)
        output = local_out + jnp.einsum('shtd,shde->shte', reaches, state, precision=highest)
        new_state = jnp.einsum('shde,shef->shdf', transit, state, precision=highest) + filled
        return (new_state, output)
    start_state = jnp.zeros((seq_count, head_count, head_size, head_size), jnp.float32)
    final_state, mixed = lax.scan(advance, start_state, moved)
    head_out = mixed.transpose(1, 0, 3, 2, 4).reshape(seq_count * tok_rows, packed).astype(jnp.bfloat16)
    group_rows = packed // N_HEAD
    total = jnp.zeros((seq_count * tok_rows, w_out.shape[1]), jnp.float32)
    for group in range(N_HEAD):
        partial_sum = jnp.dot(head_out[:, group * group_rows:(group + 1) * group_rows].astype(jnp.float32), w_out[group * group_rows:(group + 1) * group_rows].astype(jnp.float32), preferred_element_type=jnp.float32)
        total = total + partial_sum
    return total.reshape(seq_count, tok_rows, w_out.shape[1])
```

```python
import functools

import jax
import jax.numpy as jnp
from jax import lax
from jax.experimental import pallas as pl
from jax.experimental.pallas import tpu as pltpu
from jax.sharding import PartitionSpec as P

epsilon = 1e-06
f32 = jnp.float32
bf16 = jnp.bfloat16


def mm(a, b):
    return lax.dot_general(a, b, (((1,), (0,)), ((), ())), preferred_element_type=f32)


def mm_nt(a, b):
    return lax.dot_general(a, b, (((1,), (1,)), ((), ())), preferred_element_type=f32)


def mm_tn(a, b):
    return lax.dot_general(a, b, (((0,), (0,)), ((), ())), preferred_element_type=f32)


def split(x):
    high = x.astype(bf16)
    return high, (x - high.astype(f32)).astype(bf16)


def split3(x):
    high, rest = x.astype(bf16), None
    rest = x - high.astype(f32)
    middle = rest.astype(bf16)
    return high, middle, (rest - middle.astype(f32)).astype(bf16)


def dot3(a, b):
    a_high, a_low = split(a)
    b_high, b_low = split(b)
    return mm(a_high, b_high) + (mm(a_low, b_high) + mm(a_high, b_low))


def iota(shape, axis):
    return lax.broadcasted_iota(jnp.int32, shape, axis)


def local_kernel(head_count, seq, offset_ref, resets_ref, q_ref, k_ref, v_ref, gate_ref, beta_ref,
                 transit_ref, filled_ref, reach_ref, own_ref):
    tok = q_ref.shape[1]
    size = q_ref.shape[2] // head_count
    keys = 2 * tok
    half = keys // 2
    heads = range(head_count)
    offset = offset_ref[0]
    reset = [resets_ref[seq, i] for i in range(resets_ref.shape[1])]

    def doc_of(position):
        total = jnp.zeros_like(position)
        for r in reset:
            total = total + (r <= position).astype(jnp.int32)
        return total

    start_doc = sum(((r < offset).astype(jnp.int32) for r in reset), jnp.int32(0))
    last_doc = sum(((r <= offset + tok - 1).astype(jnp.int32) for r in reset), jnp.int32(0))
    doc_row = doc_of(offset + (iota((1, keys), 1) >> 1))
    doc_col = doc_of(offset + (iota((keys, 1), 0) >> 1))
    doc_tok = doc_of(offset + iota((tok, 1), 0))

    gate3 = jnp.concatenate([p.astype(f32) for p in split3(gate_ref[0])], axis=0).astype(bf16)
    beta3 = [
        jnp.concatenate([p.astype(f32) for p in split3(beta_ref[0, j])], axis=0).astype(bf16)
        for j in range(2)
    ]
    key_i, tok_i = iota((keys, tok), 0), iota((keys, tok), 1)
    running = (tok_i <= (key_i >> 1)).astype(f32).astype(bf16)
    picks = [(key_i == 2 * tok_i + j).astype(f32).astype(bf16) for j in range(2)]
    running_tok = (iota((tok, tok), 1) <= iota((tok, tok), 0)).astype(f32).astype(bf16)

    def fold_col(m):
        n = head_count
        return m[:, :n] + m[:, n:2 * n] + m[:, 2 * n:3 * n]

    def fold_row(m):
        n = head_count
        return m[:n] + m[n:2 * n] + m[2 * n:3 * n]

    gs_col = fold_col(mm_nt(running, gate3))
    gs_row = fold_row(mm_nt(gate3, running))
    gs_tok = fold_col(mm_nt(running_tok, gate3))
    beta_col = fold_col(mm_nt(picks[0], beta3[0]) + mm_nt(picks[1], beta3[1]))
    beta_row = fold_row(mm_nt(beta3[0], picks[0]) + mm_nt(beta3[1], picks[1]))

    row_i, col_i = iota((keys, keys), 0), iota((keys, keys), 1)
    below = jnp.logical_and(row_i > col_i, doc_col == doc_row)
    eye_keys = row_i == col_i
    tok_linked = jnp.logical_and(
        (iota((tok, keys), 1) >> 1) <= iota((tok, keys), 0), doc_tok == doc_row
    )
    h_i, h_j = iota((half, half), 0), iota((half, half), 1)
    apart = jnp.where(h_i > h_j, h_i ^ h_j, 0)
    eye_half = (h_i == h_j).astype(f32)
    eye_size = (iota((size, size), 0) == iota((size, size), 1)).astype(f32)

    q = [q_ref[0, :, h * size:(h + 1) * size] for h in heads]
    k = [k_ref[0, :, h * size:(h + 1) * size] for h in heads]
    v = [v_ref[0, :, h * size:(h + 1) * size] for h in heads]

    gram = [mm_nt(k[h], k[h]) for h in heads]
    q_norm = []
    for h in heads:
        q32 = q[h].astype(f32)
        q_norm.append(lax.rsqrt(jnp.sum(q32 * q32, axis=1, keepdims=True) + epsilon))
    k_col, k_row, low = [], [], []
    for h in heads:
        diag = jnp.where(eye_keys, gram[h], 0.0)
        k_col.append(lax.rsqrt(jnp.sum(diag, axis=1, keepdims=True) + epsilon))
        k_row.append(lax.rsqrt(jnp.sum(diag, axis=0, keepdims=True) + epsilon))
        spread = gs_col[:, h:h + 1] - gs_row[h:h + 1]
        left = beta_col[:, h:h + 1] * k_col[h]
        low.append(jnp.where(below, gram[h] * jnp.exp(spread) * k_row[h] * left, 0.0))

    low16 = [split(low[h]) for h in heads]
    blocks = [(h, b) for h in heads for b in range(2)]
    part = {
        (h, b): low16[h][0][b * half:(b + 1) * half, b * half:(b + 1) * half] for h, b in blocks
    }
    inv = {}
    for key in blocks:
        inv[key] = (eye_half - jnp.where(apart == 1, part[key].astype(f32), 0.0)).astype(bf16)
    width = 2
    while width < half:
        mask = jnp.logical_and(apart >= width, apart < 2 * width)
        inner = {
            key: mm(jnp.where(mask, part[key].astype(f32), 0.0).astype(bf16), inv[key]).astype(bf16)
            for key in blocks
        }
        inv = {
            key: (inv[key].astype(f32) - mm(inv[key], inner[key])).astype(bf16) for key in blocks
        }
        width *= 2
    zeros = jnp.zeros((half, half), bf16)
    first = []
    for h in heads:
        inner = mm(low16[h][0][half:, :half], inv[h, 0]).astype(bf16)
        corner = (-mm(inv[h, 1], inner)).astype(bf16)
        first.append(
            jnp.concatenate(
                [
                    jnp.concatenate([inv[h, 0], zeros], axis=1),
                    jnp.concatenate([corner, inv[h, 1]], axis=1),
                ],
                axis=0,
            )
        )
    eye32 = eye_keys.astype(f32)
    solve = []
    for h in heads:
        rest = eye32 - first[h].astype(f32) - (mm(low16[h][0], first[h]) + mm(low16[h][1], first[h]))
        solve.append(first[h].astype(f32) + mm(first[h], rest.astype(bf16)))

    for h in heads:
        gr, gc, gt = gs_row[h:h + 1], gs_col[:, h:h + 1], gs_tok[:, h:h + 1]
        carried_row = jnp.where(doc_row == start_doc, jnp.exp(gr), 0.0)
        carried_tok = jnp.where(doc_tok == start_doc, jnp.exp(gt), 0.0)
        closing = jnp.where(doc_col == last_doc, jnp.exp(gr[:, keys - 1:] - gc), 0.0)
        b_row = beta_row[h:h + 1]
        w_high, w_low = split(solve[h] * (b_row * carried_row * k_row[h]))
        u_high, u_low = split(solve[h] * b_row)
        both = jnp.concatenate(
            [mm(w_high, k[h]) + mm(w_low, k[h]), mm(u_high, v[h]) + mm(u_low, v[h])], axis=1
        )
        end_high, end_low = split(both * (closing * k_col[h]))
        ends = mm_tn(k[h], end_high) + mm_tn(k[h], end_low)
        keep = carried_row[:, keys - 1:]
        transit_ref[h] = keep * eye_size - ends[:, :size]
        filled_ref[h] = ends[:, size:]
        probes = jnp.where(
            tok_linked, mm_nt(q[h], k[h]) * jnp.exp(gt - gr) * k_row[h] * q_norm[h], 0.0
        )
        outs = dot3(probes, both)
        reach_ref[h] = (carried_tok * q_norm[h]) * q[h].astype(f32) - outs[:, :size]
        own_ref[h] = outs[:, size:]


def local_terms(seq, offset, resets, queries, keys, values, log_gate, beta):
    _, tok, packed = queries.shape
    head_count = log_gate.shape[1]
    size = packed // head_count

    def block(shape):
        return pl.BlockSpec((1,) + shape, lambda i, o, r: (seq,) + (0,) * len(shape))

    whole = pl.BlockSpec((head_count, size, size), lambda i, o, r: (0, 0, 0))
    tall = pl.BlockSpec((head_count, tok, size), lambda i, o, r: (0, 0, 0))
    return pl.pallas_call(
        functools.partial(local_kernel, head_count, seq),
        grid_spec=pltpu.PrefetchScalarGridSpec(
            num_scalar_prefetch=2,
            grid=(1,),
            in_specs=[
                block((tok, packed)),
                block((2 * tok, packed)),
                block((2 * tok, packed)),
                block((head_count, tok)),
                block((2, head_count, tok)),
            ],
            out_specs=[whole, whole, tall, tall],
        ),
        out_shape=[
            jax.ShapeDtypeStruct((head_count, size, size), f32),
            jax.ShapeDtypeStruct((head_count, size, size), f32),
            jax.ShapeDtypeStruct((head_count, tok, size), f32),
            jax.ShapeDtypeStruct((head_count, tok, size), f32),
        ],
        compiler_params=pltpu.CompilerParams(vmem_limit_bytes=48 << 20),
        name="local_terms",
    )(offset, resets, queries, keys, values, log_gate, beta)


def step_kernel(map_ref, fill_ref, state_ref, out_ref):
    for h in range(map_ref.shape[0]):
        out_ref[h] = dot3(map_ref[h], state_ref[h]) + fill_ref[h]


def step(step_map, step_fill, state):
    return pl.pallas_call(
        step_kernel,
        out_shape=jax.ShapeDtypeStruct(state.shape, f32),
        name="state_step",
    )(step_map, step_fill, state)


def project_kernel(place_ref, reach_ref, own_ref, state_ref, w_ref, send_ref, keep_ref, head_ref):
    slot = pl.program_id(0)
    heads, _, size = reach_ref.shape

    @pl.when(slot == 0)
    def _():
        for h in range(heads):
            mixed = own_ref[h] + dot3(reach_ref[h], state_ref[h])
            head_ref[:, h * size:(h + 1) * size] = mixed.astype(bf16)

    share = mm(head_ref[...], w_ref[...])

    @pl.when(slot < pl.num_programs(0) // 2)
    def _():
        send_ref[0] = share

    @pl.when(slot >= pl.num_programs(0) // 2)
    def _():
        keep_ref[0] = share


def project(groups, place, reach, own, state, w_out):
    heads, tok, size = reach.shape
    rows, width = w_out.shape
    part = width // groups
    mid = groups // 2

    def of_slot(i, p):
        r = jnp.where(i < mid, 2 * i + 1, 2 * (i - mid))
        return (0, p[0] ^ r)

    whole = pl.BlockSpec((heads, tok, size), lambda i, p: (0, 0, 0))
    square = pl.BlockSpec((heads, size, size), lambda i, p: (0, 0, 0))
    return pl.pallas_call(
        project_kernel,
        grid_spec=pltpu.PrefetchScalarGridSpec(
            num_scalar_prefetch=1,
            grid=(groups,),
            in_specs=[whole, whole, square, pl.BlockSpec((rows, part), of_slot)],
            out_specs=[
                pl.BlockSpec((1, tok, part), lambda i, p: (jnp.minimum(i, mid - 1), 0, 0)),
                pl.BlockSpec((1, tok, part), lambda i, p: (jnp.maximum(i - mid, 0), 0, 0)),
            ],
            scratch_shapes=[pltpu.VMEM((tok, heads * size), bf16)],
        ),
        out_shape=[jax.ShapeDtypeStruct((mid, tok, part), f32)] * 2,
        name="project",
    )(place, reach, own, state, w_out)


def swapped(x, axis, bit):
    size = lax.axis_size(axis)
    return lax.ppermute(x, axis, [(i, i ^ bit) for i in range(size)])


def hop(x, source):
    return lax.ppermute(x, "seq", [(source, source + 1)])


def chain(step_map, step_fill):
    devices = lax.axis_size("seq")
    if devices <= 8:
        arrived = hop(step_fill, 0)
        total = arrived
        for source in range(1, devices - 1):
            arrived = hop(step(step_map, step_fill, arrived), source)
            total = total + arrived
        return total

    def turn(_, incoming):
        return lax.ppermute(
            step(step_map, step_fill, incoming), "seq", [(i, i + 1) for i in range(devices - 1)]
        )

    return lax.fori_loop(0, devices - 1, turn, jnp.zeros_like(step_fill))


def gathered(send, keep):
    bit = 1
    while True:
        keep = keep + swapped(send, "head", bit)
        if keep.shape[0] == 1:
            return keep[0]
        send, keep = keep[1::2], keep[0::2]
        bit *= 2


def shards(queries, keys, values, log_gate, beta, resets, w_out):
    seq_count, tok, packed = queries.shape
    groups = lax.axis_size("head")
    offset = (lax.axis_index("seq") * tok).astype(jnp.int32).reshape(1)
    place = lax.axis_index("head").astype(jnp.int32).reshape(1)
    key_rows = keys.reshape(seq_count, 2 * tok, packed)
    value_rows = values.reshape(seq_count, 2 * tok, packed)
    local = [
        local_terms(s, offset, resets, queries, key_rows, value_rows, log_gate, beta)
        for s in range(seq_count)
    ]
    states = [chain(local[s][0], local[s][1]) for s in range(seq_count)]
    outs = []
    for s in range(seq_count):
        send, keep = project(groups, place, local[s][2], local[s][3], states[s], w_out)
        outs.append(gathered(send, keep))
    return jnp.stack(outs)


def solution(mesh):
    placed = (
        P("grp", "seq", "head"),
        P("grp", "seq", None, "head"),
        P("grp", "seq", None, "head"),
        P("grp", "head", "seq"),
        P("grp", None, "head", "seq"),
        P("grp", None),
        P("head", None),
    )
    return jax.shard_map(
        shards, mesh=mesh, in_specs=placed, out_specs=P("grp", "seq", "head"), check_vma=False
    )
```

```python
import functools

import jax
import jax.numpy as jnp
from jax import lax
from jax.experimental import pallas as pl
from jax.experimental.pallas import tpu as pltpu
from jax.sharding import PartitionSpec as P

epsilon = 1e-06
f32 = jnp.float32
bf16 = jnp.bfloat16


def mm(a, b):
    return lax.dot_general(a, b, (((1,), (0,)), ((), ())), preferred_element_type=f32)


def mm_nt(a, b):
    return lax.dot_general(a, b, (((1,), (1,)), ((), ())), preferred_element_type=f32)


def mm_tn(a, b):
    return lax.dot_general(a, b, (((0,), (0,)), ((), ())), preferred_element_type=f32)


def split(x):
    high = x.astype(bf16)
    return high, (x - high.astype(f32)).astype(bf16)


def split3(x):
    high, rest = x.astype(bf16), None
    rest = x - high.astype(f32)
    middle = rest.astype(bf16)
    return high, middle, (rest - middle.astype(f32)).astype(bf16)


def dot3(a, b):
    a_high, a_low = split(a)
    b_high, b_low = split(b)
    return mm(a_high, b_high) + (mm(a_low, b_high) + mm(a_high, b_low))


def iota(shape, axis):
    return lax.broadcasted_iota(jnp.int32, shape, axis)


def local_kernel(head_count, seq, offset_ref, resets_ref, q_ref, k_ref, v_ref, gate_ref, beta_ref,
                 transit_ref, filled_ref, reach_ref, own_ref):
    tok = q_ref.shape[1]
    size = q_ref.shape[2] // head_count
    keys = 2 * tok
    half = keys // 2
    heads = range(head_count)
    offset = offset_ref[0]
    reset = [resets_ref[seq, i] for i in range(resets_ref.shape[1])]

    def doc_of(position):
        total = jnp.zeros_like(position)
        for r in reset:
            total = total + (r <= position).astype(jnp.int32)
        return total

    start_doc = sum(((r < offset).astype(jnp.int32) for r in reset), jnp.int32(0))
    last_doc = sum(((r <= offset + tok - 1).astype(jnp.int32) for r in reset), jnp.int32(0))
    doc_row = doc_of(offset + (iota((1, keys), 1) >> 1))
    doc_col = doc_of(offset + (iota((keys, 1), 0) >> 1))
    doc_tok = doc_of(offset + iota((tok, 1), 0))

    gate3 = jnp.concatenate([p.astype(f32) for p in split3(gate_ref[0])], axis=0).astype(bf16)
    beta3 = [
        jnp.concatenate([p.astype(f32) for p in split3(beta_ref[0, j])], axis=0).astype(bf16)
        for j in range(2)
    ]
    key_i, tok_i = iota((keys, tok), 0), iota((keys, tok), 1)
    running = (tok_i <= (key_i >> 1)).astype(f32).astype(bf16)
    picks = [(key_i == 2 * tok_i + j).astype(f32).astype(bf16) for j in range(2)]
    running_tok = (iota((tok, tok), 1) <= iota((tok, tok), 0)).astype(f32).astype(bf16)

    def fold_col(m):
        n = head_count
        return m[:, :n] + m[:, n:2 * n] + m[:, 2 * n:3 * n]

    def fold_row(m):
        n = head_count
        return m[:n] + m[n:2 * n] + m[2 * n:3 * n]

    gs_col = fold_col(mm_nt(running, gate3))
    gs_row = fold_row(mm_nt(gate3, running))
    gs_tok = fold_col(mm_nt(running_tok, gate3))
    beta_col = fold_col(mm_nt(picks[0], beta3[0]) + mm_nt(picks[1], beta3[1]))
    beta_row = fold_row(mm_nt(beta3[0], picks[0]) + mm_nt(beta3[1], picks[1]))

    row_i, col_i = iota((keys, keys), 0), iota((keys, keys), 1)
    below = jnp.logical_and(row_i > col_i, doc_col == doc_row)
    eye_keys = row_i == col_i
    tok_linked = jnp.logical_and(
        (iota((tok, keys), 1) >> 1) <= iota((tok, keys), 0), doc_tok == doc_row
    )
    h_i, h_j = iota((half, half), 0), iota((half, half), 1)
    apart = jnp.where(h_i > h_j, h_i ^ h_j, 0)
    eye_half = (h_i == h_j).astype(f32)
    eye_size = (iota((size, size), 0) == iota((size, size), 1)).astype(f32)

    q = [q_ref[0, :, h * size:(h + 1) * size] for h in heads]
    k = [k_ref[0, :, h * size:(h + 1) * size] for h in heads]
    v = [v_ref[0, :, h * size:(h + 1) * size] for h in heads]

    gram = [mm_nt(k[h], k[h]) for h in heads]
    q_norm = []
    for h in heads:
        q32 = q[h].astype(f32)
        q_norm.append(lax.rsqrt(jnp.sum(q32 * q32, axis=1, keepdims=True) + epsilon))
    k_col, k_row, low = [], [], []
    for h in heads:
        diag = jnp.where(eye_keys, gram[h], 0.0)
        k_col.append(lax.rsqrt(jnp.sum(diag, axis=1, keepdims=True) + epsilon))
        k_row.append(lax.rsqrt(jnp.sum(diag, axis=0, keepdims=True) + epsilon))
        spread = gs_col[:, h:h + 1] - gs_row[h:h + 1]
        left = beta_col[:, h:h + 1] * k_col[h]
        low.append(jnp.where(below, gram[h] * jnp.exp(spread) * k_row[h] * left, 0.0))

    low16 = [split(low[h]) for h in heads]
    blocks = [(h, b) for h in heads for b in range(2)]
    part = {
        (h, b): low16[h][0][b * half:(b + 1) * half, b * half:(b + 1) * half] for h, b in blocks
    }
    inv = {}
    for key in blocks:
        inv[key] = (eye_half - jnp.where(apart == 1, part[key].astype(f32), 0.0)).astype(bf16)
    width = 2
    while width < half:
        mask = jnp.logical_and(apart >= width, apart < 2 * width)
        inner = {
            key: mm(jnp.where(mask, part[key].astype(f32), 0.0).astype(bf16), inv[key]).astype(bf16)
            for key in blocks
        }
        inv = {
            key: (inv[key].astype(f32) - mm(inv[key], inner[key])).astype(bf16) for key in blocks
        }
        width *= 2
    zeros = jnp.zeros((half, half), bf16)
    first = []
    for h in heads:
        inner = mm(low16[h][0][half:, :half], inv[h, 0]).astype(bf16)
        corner = (-mm(inv[h, 1], inner)).astype(bf16)
        first.append(
            jnp.concatenate(
                [
                    jnp.concatenate([inv[h, 0], zeros], axis=1),
                    jnp.concatenate([corner, inv[h, 1]], axis=1),
                ],
                axis=0,
            )
        )
    eye32 = eye_keys.astype(f32)
    solve = []
    for h in heads:
        rest = eye32 - first[h].astype(f32) - (mm(low16[h][0], first[h]) + mm(low16[h][1], first[h]))
        solve.append(first[h].astype(f32) + mm(first[h], rest.astype(bf16)))

    for h in heads:
        gr, gc, gt = gs_row[h:h + 1], gs_col[:, h:h + 1], gs_tok[:, h:h + 1]
        carried_row = jnp.where(doc_row == start_doc, jnp.exp(gr), 0.0)
        carried_tok = jnp.where(doc_tok == start_doc, jnp.exp(gt), 0.0)
        closing = jnp.where(doc_col == last_doc, jnp.exp(gr[:, keys - 1:] - gc), 0.0)
        b_row = beta_row[h:h + 1]
        w_high, w_low = split(solve[h] * (b_row * carried_row * k_row[h]))
        u_high, u_low = split(solve[h] * b_row)
        both = jnp.concatenate(
            [mm(w_high, k[h]) + mm(w_low, k[h]), mm(u_high, v[h]) + mm(u_low, v[h])], axis=1
        )
        end_high, end_low = split(both * (closing * k_col[h]))
        ends = mm_tn(k[h], end_high) + mm_tn(k[h], end_low)
        keep = carried_row[:, keys - 1:]
        transit_ref[h] = keep * eye_size - ends[:, :size]
        filled_ref[h] = ends[:, size:]
        probes = jnp.where(
            tok_linked, mm_nt(q[h], k[h]) * jnp.exp(gt - gr) * k_row[h] * q_norm[h], 0.0
        )
        outs = dot3(probes, both)
        reach_ref[h] = (carried_tok * q_norm[h]) * q[h].astype(f32) - outs[:, :size]
        own_ref[h] = outs[:, size:]


def local_terms(seq, offset, resets, queries, keys, values, log_gate, beta):
    _, tok, packed = queries.shape
    head_count = log_gate.shape[1]
    size = packed // head_count

    def block(shape):
        return pl.BlockSpec((1,) + shape, lambda i, o, r: (seq,) + (0,) * len(shape))

    whole = pl.BlockSpec((head_count, size, size), lambda i, o, r: (0, 0, 0))
    tall = pl.BlockSpec((head_count, tok, size), lambda i, o, r: (0, 0, 0))
    return pl.pallas_call(
        functools.partial(local_kernel, head_count, seq),
        grid_spec=pltpu.PrefetchScalarGridSpec(
            num_scalar_prefetch=2,
            grid=(1,),
            in_specs=[
                block((tok, packed)),
                block((2 * tok, packed)),
                block((2 * tok, packed)),
                block((head_count, tok)),
                block((2, head_count, tok)),
            ],
            out_specs=[whole, whole, tall, tall],
        ),
        out_shape=[
            jax.ShapeDtypeStruct((head_count, size, size), f32),
            jax.ShapeDtypeStruct((head_count, size, size), f32),
            jax.ShapeDtypeStruct((head_count, tok, size), f32),
            jax.ShapeDtypeStruct((head_count, tok, size), f32),
        ],
        compiler_params=pltpu.CompilerParams(vmem_limit_bytes=16 << 20),
        name="local_terms",
    )(offset, resets, queries, keys, values, log_gate, beta)


def vmem(count):
    return [pl.BlockSpec(memory_space=pltpu.VMEM)] * count


def step_kernel(choices, here_ref, *refs):
    maps, fills = refs[:choices], refs[choices:2 * choices]
    state_ref, out_ref = refs[2 * choices:]
    here = here_ref[0]
    for n in range(choices):

        @pl.when(here == n)
        def _(n=n):
            for h in range(state_ref.shape[0]):
                out_ref[h] = dot3(maps[n][h], state_ref[h]) + fills[n][h]

    @pl.when(jnp.logical_or(here < 0, here >= choices))
    def _():
        out_ref[...] = fills[0][...]


def step(here, maps, fills, state):
    return pl.pallas_call(
        functools.partial(step_kernel, len(maps)),
        in_specs=[pl.BlockSpec(memory_space=pltpu.SMEM)] + vmem(2 * len(maps) + 1),
        out_specs=pl.BlockSpec(memory_space=pltpu.VMEM),
        out_shape=jax.ShapeDtypeStruct(state.shape, f32),
        compiler_params=pltpu.CompilerParams(vmem_limit_bytes=8 << 20),
        name="state_step",
    )(here, *maps, *fills, state)


def project_kernel(choices, groups, here_ref, place_ref, reach_ref, own_ref, *refs):
    states = refs[:choices]
    w_ref, send_ref, keep_ref, head_ref, state_ref = refs[choices:]
    heads, _, size = reach_ref.shape
    here, place = here_ref[0], place_ref[0]
    part = w_ref.shape[1] // groups

    @pl.when(here == 0)
    def _():
        for h in range(heads):
            head_ref[:, h * size:(h + 1) * size] = own_ref[h].astype(bf16)

    @pl.when(here > 0)
    def _():
        for n in range(choices):

            @pl.when(here == n + 1)
            def _(n=n):
                state_ref[...] = states[n][...]

        for h in range(heads):
            mixed = own_ref[h] + dot3(reach_ref[h], state_ref[h])
            head_ref[:, h * size:(h + 1) * size] = mixed.astype(bf16)

    for r in range(groups):
        start = pl.multiple_of((place ^ r) * part, part)
        share = mm(head_ref[...], w_ref[:, pl.ds(start, part)])
        if r % 2:
            send_ref[r // 2] = share
        else:
            keep_ref[r // 2] = share


def project(groups, here, place, reach, own, states, w_out):
    heads, tok, size = reach.shape
    part = w_out.shape[1] // groups
    smem = pl.BlockSpec(memory_space=pltpu.SMEM)
    return pl.pallas_call(
        functools.partial(project_kernel, len(states), groups),
        in_specs=[smem, smem] + vmem(3 + len(states)),
        out_specs=vmem(2),
        out_shape=[jax.ShapeDtypeStruct((groups // 2, tok, part), f32)] * 2,
        scratch_shapes=[
            pltpu.VMEM((tok, heads * size), bf16),
            pltpu.VMEM((heads, size, size), f32),
        ],
        compiler_params=pltpu.CompilerParams(vmem_limit_bytes=16 << 20),
        name="project",
    )(here, place, reach, own, *states, w_out)


def after(small, *arrays):
    return lax.optimization_barrier((small,) + arrays)[0]


def swapped(x, axis, bit):
    size = lax.axis_size(axis)
    return lax.ppermute(x, axis, [(i, i ^ bit) for i in range(size)])


def carry_on(devices, x, round_index, chunks):
    pairs = [(i, i + 1) for i in range(devices - 1) if 0 <= round_index - i < chunks]
    return lax.ppermute(x, "seq", pairs)


def gathered(keep, received):
    keep = keep + received
    bit = 2
    while keep.shape[0] > 1:
        keep = keep[0::2] + swapped(keep[1::2], "head", bit)
        bit *= 2
    return keep[0]


def shards(queries, keys, values, log_gate, beta, resets, w_out):
    chunks, tok, packed = queries.shape
    groups = lax.axis_size("head")
    devices = lax.axis_size("seq")
    here = lax.axis_index("seq").astype(jnp.int32).reshape(1)
    offset = here * tok
    place = lax.axis_index("head").astype(jnp.int32).reshape(1)
    key_rows = keys.reshape(chunks, 2 * tok, packed)
    value_rows = values.reshape(chunks, 2 * tok, packed)

    def local(s, offset):
        return local_terms(s, offset, resets, queries, key_rows, value_rows, log_gate, beta)

    if devices > 8:
        terms = [local(s, offset) for s in range(chunks)]
        pairs = [(i, i + 1) for i in range(devices - 1)]
        no_choice = jnp.zeros((1,), jnp.int32)

        def turn(_, incoming):
            return tuple(
                lax.ppermute(
                    step(no_choice, [terms[s][0]], [terms[s][1]], incoming[s]), "seq", pairs
                )
                for s in range(chunks)
            )

        zero = tuple(jnp.zeros_like(terms[s][1]) for s in range(chunks))
        states = lax.fori_loop(0, devices - 1, turn, zero)
        outs = []
        for s in range(chunks):
            one = jnp.ones((1,), jnp.int32)
            send, keep = project(groups, one, place, terms[s][2], terms[s][3], [states[s]], w_out)
            outs.append(gathered(keep, swapped(send, "head", 1)))
        return jnp.stack(outs)

    last_round = chunks + devices - 3
    terms, arrived, outs = [], [], []
    token = None
    for r in range(last_round + devices):
        if r < chunks:
            terms.append(local(r, offset if token is None else after(offset, token)))
            token = terms[r][1]
        done = r - devices + 1
        if r <= last_round:
            if r == 0:
                sent = terms[0][1]
            else:
                valid = [r - i for i in range(devices - 1) if 0 <= r - i < chunks]
                first = r - valid[0]
                sent = step(
                    after(here - first, token),
                    [terms[c][0] for c in valid],
                    [terms[c][1] for c in valid],
                    arrived[r - 1],
                )
                token = sent
            arrived.append(carry_on(devices, sent, r, chunks))
        if 0 <= done < chunks:
            send, keep = project(
                groups, after(here, token), place, terms[done][2], terms[done][3],
                [arrived[done + i] for i in range(devices - 1)], w_out,
            )
            token = keep
            outs.append(gathered(keep, swapped(send, "head", 1)))
    return jnp.stack(outs)


def solution(mesh):
    placed = (
        P("grp", "seq", "head"),
        P("grp", "seq", None, "head"),
        P("grp", "seq", None, "head"),
        P("grp", "head", "seq"),
        P("grp", None, "head", "seq"),
        P("grp", None),
        P("head", None),
    )
    return jax.shard_map(
        shards, mesh=mesh, in_specs=placed, out_specs=P("grp", "seq", "head"), check_vma=False
    )
```

```python
import functools

import jax
import jax.numpy as jnp
from jax import lax
from jax.experimental import pallas as pl
from jax.experimental.pallas import tpu as pltpu
from jax.sharding import PartitionSpec as P

epsilon = 1e-06
small_cost = pl.CostEstimate(flops=1 << 20, transcendentals=0, bytes_accessed=1 << 10)
f32 = jnp.float32
bf16 = jnp.bfloat16


def mm(a, b):
    return lax.dot_general(a, b, (((1,), (0,)), ((), ())), preferred_element_type=f32)


def mm_nt(a, b):
    return lax.dot_general(a, b, (((1,), (1,)), ((), ())), preferred_element_type=f32)


def mm_tn(a, b):
    return lax.dot_general(a, b, (((0,), (0,)), ((), ())), preferred_element_type=f32)


def split(x):
    high = x.astype(bf16)
    return high, (x - high.astype(f32)).astype(bf16)


def split3(x):
    high, rest = x.astype(bf16), None
    rest = x - high.astype(f32)
    middle = rest.astype(bf16)
    return high, middle, (rest - middle.astype(f32)).astype(bf16)


def dot3(a, b):
    a_high, a_low = split(a)
    b_high, b_low = split(b)
    return mm(a_high, b_high) + (mm(a_low, b_high) + mm(a_high, b_low))


def iota(shape, axis):
    return lax.broadcasted_iota(jnp.int32, shape, axis)


def local_kernel(head_count, seq, offset_ref, resets_ref, q_ref, k_ref, v_ref, gate_ref, beta_ref,
                 *refs):
    transit_ref, filled_ref, reach_ref, own_ref = refs[-4:]
    tok = q_ref.shape[1]
    size = q_ref.shape[2] // head_count
    keys = 2 * tok
    half = keys // 2
    heads = range(head_count)
    offset = offset_ref[0]
    reset = [resets_ref[seq, i] for i in range(resets_ref.shape[1])]

    def doc_of(position):
        total = jnp.zeros_like(position)
        for r in reset:
            total = total + (r <= position).astype(jnp.int32)
        return total

    start_doc = sum(((r < offset).astype(jnp.int32) for r in reset), jnp.int32(0))
    last_doc = sum(((r <= offset + tok - 1).astype(jnp.int32) for r in reset), jnp.int32(0))
    doc_row = doc_of(offset + (iota((1, keys), 1) >> 1))
    doc_col = doc_of(offset + (iota((keys, 1), 0) >> 1))
    doc_tok = doc_of(offset + iota((tok, 1), 0))

    def stacked(x):
        return jnp.concatenate([p.astype(f32) for p in split3(x)], axis=0).astype(bf16)

    def folded(m):
        n = head_count
        return m[:n] + m[n:2 * n] + m[2 * n:3 * n]

    tok_i, key_i = iota((tok, keys), 0), iota((tok, keys), 1)
    gate3 = stacked(gate_ref[0])
    gs_row = folded(mm(gate3, (tok_i <= (key_i >> 1)).astype(f32).astype(bf16)))
    beta_row = folded(
        mm(stacked(beta_ref[0, 0]), (key_i == 2 * tok_i).astype(f32).astype(bf16))
        + mm(stacked(beta_ref[0, 1]), (key_i == 2 * tok_i + 1).astype(f32).astype(bf16))
    )
    gs_tok_row = folded(
        mm(gate3, (iota((tok, tok), 0) <= iota((tok, tok), 1)).astype(f32).astype(bf16))
    )
    gs_col, beta_col, gs_tok = gs_row.T, beta_row.T, gs_tok_row.T

    h_i, h_j = iota((half, half), 0), iota((half, half), 1)
    eye_half = h_i == h_j
    apart = jnp.where(h_i > h_j, h_i ^ h_j, 0)
    widths = [1 << n for n in range((half - 1).bit_length())]
    masks = [
        jnp.logical_and(apart >= w, apart < 2 * w).astype(f32).astype(bf16) for w in widths
    ]
    eye16 = eye_half.astype(f32).astype(bf16)
    eye_size = (iota((size, size), 0) == iota((size, size), 1)).astype(f32)
    top_mask = jnp.logical_and(h_i > h_j, doc_col[:half] == doc_row[:, :half])
    low_i, low_j = iota((half, keys), 0), iota((half, keys), 1)
    bottom_mask = jnp.logical_and(low_i + half > low_j, doc_col[half:] == doc_row)
    tok_linked = jnp.logical_and(
        (iota((tok, keys), 1) >> 1) <= iota((tok, keys), 0), doc_tok == doc_row
    )

    q = [q_ref[0, :, h * size:(h + 1) * size] for h in heads]
    k = [k_ref[0, :, h * size:(h + 1) * size] for h in heads]
    v = [v_ref[0, :, h * size:(h + 1) * size] for h in heads]

    def unit(x):
        return lax.rsqrt(jnp.sum(x * x, axis=1, keepdims=True) + epsilon)

    top, bottom, k_col, k_row, right = [], [], [], [], []
    for h in heads:
        gram_top = mm_nt(k[h][:half], k[h][:half])
        gram_bottom = mm_nt(k[h][half:], k[h])
        k32 = k[h].astype(f32)
        k_col.append(unit(k32))
        squares = jnp.concatenate(
            [
                jnp.sum(jnp.where(eye_half, g, 0.0), axis=0, keepdims=True)
                for g in (gram_top, gram_bottom[:, half:])
            ],
            axis=1,
        )
        k_row.append(lax.rsqrt(squares + epsilon))
        gr, gc = gs_row[h:h + 1], gs_col[:, h:h + 1]
        b_col = beta_col[:, h:h + 1]
        left = b_col * k_col[h]
        carried = jnp.where(doc_col == start_doc, jnp.exp(gc), 0.0)
        right.append(
            jnp.concatenate([k32 * (left * carried), v[h].astype(f32) * b_col], axis=1)
        )
        top.append(
            split(
                jnp.where(
                    top_mask,
                    gram_top * jnp.exp(gc[:half] - gr[:, :half]) * k_row[h][:, :half] * left[:half],
                    0.0,
                )
            )
        )
        bottom.append(
            split(
                jnp.where(
                    bottom_mask, gram_bottom * jnp.exp(gc[half:] - gr) * k_row[h] * left[half:], 0.0
                )
            )
        )

    blocks = [(h, b) for h in heads for b in range(2)]
    part = {(h, b): top[h][0] if b == 0 else bottom[h][0][:, half:] for h, b in blocks}
    inv = {key: eye16 - part[key] * masks[0] for key in blocks}
    for mask in masks[1:]:
        inner = {key: mm(part[key] * mask, inv[key]).astype(bf16) for key in blocks}
        inv = {key: inv[key] - mm(inv[key], inner[key]).astype(bf16) for key in blocks}
    lower = []
    for h in heads:
        inner = mm(bottom[h][0][:, :half], inv[h, 0]).astype(bf16)
        lower.append(
            jnp.concatenate([-mm(inv[h, 1], inner).astype(bf16), inv[h, 1]], axis=1)
        )

    both = []
    for h in heads:
        rough = right[h].astype(bf16)
        g_top = mm(inv[h, 0], rough[:half]).astype(bf16)
        g_bottom = mm(lower[h], rough).astype(bf16)
        guess = jnp.concatenate([g_top, g_bottom], axis=0)
        rest_top = right[h][:half] - g_top.astype(f32) - (
            mm(top[h][0], g_top) + mm(top[h][1], g_top)
        )
        rest_bottom = right[h][half:] - g_bottom.astype(f32) - (
            mm(bottom[h][0], guess) + mm(bottom[h][1], guess)
        )
        rest = jnp.concatenate([rest_top.astype(bf16), rest_bottom.astype(bf16)], axis=0)
        both.append(
            jnp.concatenate(
                [
                    g_top.astype(f32) + mm(inv[h, 0], rest[:half]),
                    g_bottom.astype(f32) + mm(lower[h], rest),
                ],
                axis=0,
            )
        )

    for h in heads:
        gr, gc, gt = gs_row[h:h + 1], gs_col[:, h:h + 1], gs_tok[:, h:h + 1]
        last = gr[:, keys - 1:]
        carried_tok = jnp.where(doc_tok == start_doc, jnp.exp(gt), 0.0)
        closing = jnp.where(doc_col == last_doc, jnp.exp(last - gc), 0.0)
        end_high, end_low = split(both[h] * (closing * k_col[h]))
        ends = mm_tn(k[h], end_high) + mm_tn(k[h], end_low)
        keep = jnp.where(last_doc == start_doc, jnp.exp(last), 0.0)
        transit_ref[h] = keep * eye_size - ends[:, :size]
        filled_ref[h] = ends[:, size:]
        q32 = q[h].astype(f32)
        q_norm = unit(q32)
        probes = jnp.where(
            tok_linked, mm_nt(q[h], k[h]) * jnp.exp(gt - gr) * k_row[h] * q_norm, 0.0
        )
        outs = dot3(probes, both[h])
        reach_ref[h] = (carried_tok * q_norm) * q32 - outs[:, :size]
        own_ref[h] = outs[:, size:]


def local_terms(seq, offset, resets, queries, keys, values, log_gate, beta, earlier=()):
    _, tok, packed = queries.shape
    head_count = log_gate.shape[1]
    size = packed // head_count

    def block(shape):
        return pl.BlockSpec((1,) + shape, lambda i, o, r: (seq,) + (0,) * len(shape))

    whole = pl.BlockSpec((head_count, size, size), lambda i, o, r: (0, 0, 0))
    tall = pl.BlockSpec((head_count, tok, size), lambda i, o, r: (0, 0, 0))
    return pl.pallas_call(
        functools.partial(local_kernel, head_count, seq),
        grid_spec=pltpu.PrefetchScalarGridSpec(
            num_scalar_prefetch=2,
            grid=(1,),
            in_specs=[
                block((tok, packed)),
                block((2 * tok, packed)),
                block((2 * tok, packed)),
                block((head_count, tok)),
                block((2, head_count, tok)),
            ]
            + untouched(earlier),
            out_specs=[whole, whole, tall, tall],
        ),
        out_shape=[
            jax.ShapeDtypeStruct((head_count, size, size), f32),
            jax.ShapeDtypeStruct((head_count, size, size), f32),
            jax.ShapeDtypeStruct((head_count, tok, size), f32),
            jax.ShapeDtypeStruct((head_count, tok, size), f32),
        ],
        compiler_params=pltpu.CompilerParams(vmem_limit_bytes=16 << 20),
        name="local_terms",
    )(offset, resets, queries, keys, values, log_gate, beta, *earlier)


def vmem(count):
    return [pl.BlockSpec(memory_space=pltpu.VMEM)] * count


def untouched(earlier):
    return [pl.BlockSpec(memory_space=pl.ANY)] * len(earlier)


def step_kernel(choices, here_ref, *refs):
    maps, fills, state_ref, out_ref = refs[:choices], refs[choices:2 * choices], refs[2 * choices], refs[-1]
    here = here_ref[0]
    for n in range(choices):

        @pl.when(here == n)
        def _(n=n):
            for h in range(state_ref.shape[0]):
                out_ref[h] = dot3(maps[n][h], state_ref[h]) + fills[n][h]

    @pl.when(jnp.logical_or(here < 0, here >= choices))
    def _():
        out_ref[...] = fills[0][...]


def step(here, maps, fills, state, earlier=()):
    return pl.pallas_call(
        functools.partial(step_kernel, len(maps)),
        in_specs=[pl.BlockSpec(memory_space=pltpu.SMEM)]
        + vmem(2 * len(maps) + 1)
        + untouched(earlier),
        out_specs=pl.BlockSpec(memory_space=pltpu.VMEM),
        out_shape=jax.ShapeDtypeStruct(state.shape, f32),
        compiler_params=pltpu.CompilerParams(vmem_limit_bytes=8 << 20),
        cost_estimate=small_cost,
        name="state_step",
    )(here, *maps, *fills, state, *earlier)


def project_kernel(choices, groups, here_ref, place_ref, reach_ref, own_ref, *refs):
    states, w_ref = refs[:choices], refs[choices]
    send_ref, keep_ref, head_ref, state_ref = refs[-4:]
    heads, _, size = reach_ref.shape
    here, place = here_ref[0], place_ref[0]
    part = w_ref.shape[1] // groups

    @pl.when(here == 0)
    def _():
        for h in range(heads):
            head_ref[:, h * size:(h + 1) * size] = own_ref[h].astype(bf16)

    @pl.when(here > 0)
    def _():
        for n in range(choices):

            @pl.when(here == n + 1)
            def _(n=n):
                state_ref[...] = states[n][...]

        for h in range(heads):
            mixed = own_ref[h] + dot3(reach_ref[h], state_ref[h])
            head_ref[:, h * size:(h + 1) * size] = mixed.astype(bf16)

    for r in range(groups):
        start = pl.multiple_of((place ^ r) * part, part)
        share = mm(head_ref[...], w_ref[:, pl.ds(start, part)])
        if r % 2:
            send_ref[r // 2] = share
        else:
            keep_ref[r // 2] = share


def project(groups, here, place, reach, own, states, w_out, earlier=()):
    heads, tok, size = reach.shape
    part = w_out.shape[1] // groups
    smem = pl.BlockSpec(memory_space=pltpu.SMEM)
    return pl.pallas_call(
        functools.partial(project_kernel, len(states), groups),
        in_specs=[smem, smem] + vmem(3 + len(states)) + untouched(earlier),
        out_specs=vmem(2),
        out_shape=[jax.ShapeDtypeStruct((groups // 2, tok, part), f32)] * 2,
        scratch_shapes=[
            pltpu.VMEM((tok, heads * size), bf16),
            pltpu.VMEM((heads, size, size), f32),
        ],
        compiler_params=pltpu.CompilerParams(vmem_limit_bytes=16 << 20),
        cost_estimate=small_cost,
        name="project",
    )(here, place, reach, own, *states, w_out, *earlier)


def swapped(x, axis, bit):
    size = lax.axis_size(axis)
    return lax.ppermute(x, axis, [(i, i ^ bit) for i in range(size)])


def carry_on(devices, x, round_index, chunks):
    pairs = [(i, i + 1) for i in range(devices - 1) if 0 <= round_index - i < chunks]
    return lax.ppermute(x, "seq", pairs)


def add_kernel(mine_ref, other_ref, *refs):
    leave_ref, stay_ref = refs[-2:]
    for r in range(mine_ref.shape[0]):
        out_ref = leave_ref if r % 2 else stay_ref
        out_ref[r // 2] = mine_ref[r] + other_ref[r]


def add_parts(mine, other, earlier=()):
    part = jax.ShapeDtypeStruct((mine.shape[0] // 2,) + mine.shape[1:], f32)
    return pl.pallas_call(
        add_kernel,
        in_specs=vmem(2) + untouched(earlier),
        out_specs=vmem(2),
        out_shape=[part] * 2,
        compiler_params=pltpu.CompilerParams(vmem_limit_bytes=4 << 20),
        cost_estimate=small_cost,
        name="add_parts",
    )(mine, other, *earlier)


def reduced(send, keep):
    bit = 2
    while True:
        other = swapped(send, "head", bit)
        if keep.shape[0] == 1:
            return keep[0], other[0]
        send, keep = add_parts(keep, other)
        bit *= 2


def shards(queries, keys, values, log_gate, beta, resets, w_out):
    chunks, tok, packed = queries.shape
    groups = lax.axis_size("head")
    devices = lax.axis_size("seq")
    here = lax.axis_index("seq").astype(jnp.int32).reshape(1)
    offset = here * tok
    place = lax.axis_index("head").astype(jnp.int32).reshape(1)
    key_rows = keys.reshape(chunks, 2 * tok, packed)
    value_rows = values.reshape(chunks, 2 * tok, packed)

    def local(s, earlier=()):
        return local_terms(
            s, offset, resets, queries, key_rows, value_rows, log_gate, beta, earlier
        )

    if devices > 8:
        terms = [local(s) for s in range(chunks)]
        pairs = [(i, i + 1) for i in range(devices - 1)]
        no_choice = jnp.zeros((1,), jnp.int32)

        def turn(_, incoming):
            return tuple(
                lax.ppermute(
                    step(no_choice, [terms[s][0]], [terms[s][1]], incoming[s]), "seq", pairs
                )
                for s in range(chunks)
            )

        zero = tuple(jnp.zeros_like(terms[s][1]) for s in range(chunks))
        states = lax.fori_loop(0, devices - 1, turn, zero)
        outs = []
        for s in range(chunks):
            one = jnp.ones((1,), jnp.int32)
            send, keep = project(groups, one, place, terms[s][2], terms[s][3], [states[s]], w_out)
            leave, stay = add_parts(keep, swapped(send, "head", 1))
            outs.append(reduced(leave, stay))
        return jnp.stack([mine + other for mine, other in outs])

    last_round = chunks + devices - 3
    terms, arrived, outs = [], [], []
    token = ()
    for r in range(last_round + devices):
        if r < chunks:
            terms.append(local(r, token))
            token = (terms[r][1],)
        done = r - devices + 1
        if r <= last_round:
            if r == 0:
                sent = terms[0][1]
            else:
                valid = [r - i for i in range(devices - 1) if 0 <= r - i < chunks]
                sent = step(
                    here - (r - valid[0]),
                    [terms[c][0] for c in valid],
                    [terms[c][1] for c in valid],
                    arrived[r - 1],
                    token,
                )
                token = (sent,)
            arrived.append(carry_on(devices, sent, r, chunks))
        if 0 <= done < chunks:
            settled = (outs[done - 2][1],) if done >= 2 else ()
            send, keep = project(
                groups, here, place, terms[done][2], terms[done][3],
                [arrived[done + i] for i in range(devices - 1)], w_out, token + settled,
            )
            leave, stay = add_parts(keep, swapped(send, "head", 1), token)
            token = (leave,)
            outs.append(reduced(leave, stay))
    return jnp.stack([mine + other for mine, other in outs])


def solution(mesh):
    placed = (
        P("grp", "seq", "head"),
        P("grp", "seq", None, "head"),
        P("grp", "seq", None, "head"),
        P("grp", "head", "seq"),
        P("grp", None, "head", "seq"),
        P("grp", None),
        P("head", None),
    )
    return jax.shard_map(
        shards, mesh=mesh, in_specs=placed, out_specs=P("grp", "seq", "head"), check_vma=False
    )
```

```python
import functools

import jax
import jax.numpy as jnp
from jax import lax
from jax.experimental import pallas as pl
from jax.experimental.pallas import tpu as pltpu
from jax.sharding import PartitionSpec as P

epsilon = 1e-06
small_cost = pl.CostEstimate(flops=1 << 20, transcendentals=0, bytes_accessed=1 << 10)
f32 = jnp.float32
bf16 = jnp.bfloat16


def mm(a, b):
    return lax.dot_general(a, b, (((1,), (0,)), ((), ())), preferred_element_type=f32)


def mm_nt(a, b):
    return lax.dot_general(a, b, (((1,), (1,)), ((), ())), preferred_element_type=f32)


def mm_tn(a, b):
    return lax.dot_general(a, b, (((0,), (0,)), ((), ())), preferred_element_type=f32)


def split(x):
    high = x.astype(bf16)
    return high, (x - high.astype(f32)).astype(bf16)


def split3(x):
    high, rest = x.astype(bf16), None
    rest = x - high.astype(f32)
    middle = rest.astype(bf16)
    return high, middle, (rest - middle.astype(f32)).astype(bf16)


def dot3(a, b):
    a_high, a_low = split(a)
    b_high, b_low = split(b)
    return mm(a_high, b_high) + (mm(a_low, b_high) + mm(a_high, b_low))


def iota(shape, axis):
    return lax.broadcasted_iota(jnp.int32, shape, axis)


def local_kernel(head_count, seq, offset_ref, resets_ref, q_ref, k_ref, v_ref, gate_ref, beta_ref,
                 *refs):
    transit_ref, filled_ref, reach_ref, own_ref = refs[-4:]
    tok = q_ref.shape[1]
    size = q_ref.shape[2] // head_count
    keys = 2 * tok
    half = keys // 2
    heads = range(head_count)
    offset = offset_ref[0]
    reset = [resets_ref[seq, i] for i in range(resets_ref.shape[1])]

    def doc_of(position):
        total = jnp.zeros_like(position)
        for r in reset:
            total = total + (r <= position).astype(jnp.int32)
        return total

    start_doc = sum(((r < offset).astype(jnp.int32) for r in reset), jnp.int32(0))
    last_doc = sum(((r <= offset + tok - 1).astype(jnp.int32) for r in reset), jnp.int32(0))
    doc_row = doc_of(offset + (iota((1, keys), 1) >> 1))
    doc_col = doc_of(offset + (iota((keys, 1), 0) >> 1))
    doc_tok = doc_of(offset + iota((tok, 1), 0))

    def stacked(x):
        return jnp.concatenate([p.astype(f32) for p in split3(x)], axis=0).astype(bf16)

    def folded(m):
        n = head_count
        return m[:n] + m[n:2 * n] + m[2 * n:3 * n]

    tok_i, key_i = iota((tok, keys), 0), iota((tok, keys), 1)
    gate3 = stacked(gate_ref[0])
    gs_row = folded(mm(gate3, (tok_i <= (key_i >> 1)).astype(f32).astype(bf16)))
    beta_row = folded(
        mm(stacked(beta_ref[0, 0]), (key_i == 2 * tok_i).astype(f32).astype(bf16))
        + mm(stacked(beta_ref[0, 1]), (key_i == 2 * tok_i + 1).astype(f32).astype(bf16))
    )
    gs_tok_row = folded(
        mm(gate3, (iota((tok, tok), 0) <= iota((tok, tok), 1)).astype(f32).astype(bf16))
    )
    gs_col, beta_col, gs_tok = gs_row.T, beta_row.T, gs_tok_row.T

    h_i, h_j = iota((half, half), 0), iota((half, half), 1)
    eye_half = h_i == h_j
    apart = jnp.where(h_i > h_j, h_i ^ h_j, 0)
    widths = [1 << n for n in range((half - 1).bit_length())]
    masks = [
        jnp.logical_and(apart >= w, apart < 2 * w).astype(f32).astype(bf16) for w in widths
    ]
    eye16 = eye_half.astype(f32).astype(bf16)
    eye_size = (iota((size, size), 0) == iota((size, size), 1)).astype(f32)
    top_mask = jnp.logical_and(h_i > h_j, doc_col[:half] == doc_row[:, :half])
    low_i, low_j = iota((half, keys), 0), iota((half, keys), 1)
    bottom_mask = jnp.logical_and(low_i + half > low_j, doc_col[half:] == doc_row)
    tok_linked = jnp.logical_and(
        (iota((tok, keys), 1) >> 1) <= iota((tok, keys), 0), doc_tok == doc_row
    )

    q = [q_ref[0, :, h * size:(h + 1) * size] for h in heads]
    k = [k_ref[0, :, h * size:(h + 1) * size] for h in heads]
    v = [v_ref[0, :, h * size:(h + 1) * size] for h in heads]

    def unit(x):
        return lax.rsqrt(jnp.sum(x * x, axis=1, keepdims=True) + epsilon)

    top, bottom, k_col, k_row, right = [], [], [], [], []
    for h in heads:
        gram_top = mm_nt(k[h][:half], k[h][:half])
        gram_bottom = mm_nt(k[h][half:], k[h])
        k32 = k[h].astype(f32)
        k_col.append(unit(k32))
        squares = jnp.concatenate(
            [
                jnp.sum(jnp.where(eye_half, g, 0.0), axis=0, keepdims=True)
                for g in (gram_top, gram_bottom[:, half:])
            ],
            axis=1,
        )
        k_row.append(lax.rsqrt(squares + epsilon))
        gr, gc = gs_row[h:h + 1], gs_col[:, h:h + 1]
        b_col = beta_col[:, h:h + 1]
        left = b_col * k_col[h]
        carried = jnp.where(doc_col == start_doc, jnp.exp(gc), 0.0)
        right.append(
            jnp.concatenate([k32 * (left * carried), v[h].astype(f32) * b_col], axis=1)
        )
        top.append(
            split(
                jnp.where(
                    top_mask,
                    gram_top * jnp.exp(gc[:half] - gr[:, :half]) * k_row[h][:, :half] * left[:half],
                    0.0,
                )
            )
        )
        bottom.append(
            split(
                jnp.where(
                    bottom_mask, gram_bottom * jnp.exp(gc[half:] - gr) * k_row[h] * left[half:], 0.0
                )
            )
        )

    blocks = [(h, b) for h in heads for b in range(2)]
    part = {(h, b): top[h][0] if b == 0 else bottom[h][0][:, half:] for h, b in blocks}
    inv = {key: eye16 - part[key] * masks[0] for key in blocks}
    for mask in masks[1:]:
        inner = {key: mm(part[key] * mask, inv[key]).astype(bf16) for key in blocks}
        inv = {key: inv[key] - mm(inv[key], inner[key]).astype(bf16) for key in blocks}
    lower = []
    for h in heads:
        inner = mm(bottom[h][0][:, :half], inv[h, 0]).astype(bf16)
        lower.append(
            jnp.concatenate([-mm(inv[h, 1], inner).astype(bf16), inv[h, 1]], axis=1)
        )

    both = []
    for h in heads:
        rough = right[h].astype(bf16)
        g_top = mm(inv[h, 0], rough[:half]).astype(bf16)
        g_bottom = mm(lower[h], rough).astype(bf16)
        guess = jnp.concatenate([g_top, g_bottom], axis=0)
        rest_top = right[h][:half] - g_top.astype(f32) - (
            mm(top[h][0], g_top) + mm(top[h][1], g_top)
        )
        rest_bottom = right[h][half:] - g_bottom.astype(f32) - (
            mm(bottom[h][0], guess) + mm(bottom[h][1], guess)
        )
        rest = jnp.concatenate([rest_top.astype(bf16), rest_bottom.astype(bf16)], axis=0)
        both.append(
            jnp.concatenate(
                [
                    g_top.astype(f32) + mm(inv[h, 0], rest[:half]),
                    g_bottom.astype(f32) + mm(lower[h], rest),
                ],
                axis=0,
            )
        )

    for h in heads:
        gr, gc, gt = gs_row[h:h + 1], gs_col[:, h:h + 1], gs_tok[:, h:h + 1]
        last = gr[:, keys - 1:]
        carried_tok = jnp.where(doc_tok == start_doc, jnp.exp(gt), 0.0)
        closing = jnp.where(doc_col == last_doc, jnp.exp(last - gc), 0.0)
        end_high, end_low = split(both[h] * (closing * k_col[h]))
        ends = mm_tn(k[h], end_high) + mm_tn(k[h], end_low)
        keep = jnp.where(last_doc == start_doc, jnp.exp(last), 0.0)
        transit_ref[h] = keep * eye_size - ends[:, :size]
        filled_ref[h] = ends[:, size:]
        q32 = q[h].astype(f32)
        q_norm = unit(q32)
        probes = jnp.where(
            tok_linked, mm_nt(q[h], k[h]) * jnp.exp(gt - gr) * k_row[h] * q_norm, 0.0
        )
        outs = dot3(probes, both[h])
        reach_ref[h] = (carried_tok * q_norm) * q32 - outs[:, :size]
        own_ref[h] = outs[:, size:]


def local_terms(seq, offset, resets, queries, keys, values, log_gate, beta, earlier=()):
    _, tok, packed = queries.shape
    head_count = log_gate.shape[1]
    size = packed // head_count

    def block(shape):
        return pl.BlockSpec((1,) + shape, lambda i, o, r: (seq,) + (0,) * len(shape))

    whole = pl.BlockSpec((head_count, size, size), lambda i, o, r: (0, 0, 0))
    tall = pl.BlockSpec((head_count, tok, size), lambda i, o, r: (0, 0, 0))
    return pl.pallas_call(
        functools.partial(local_kernel, head_count, seq),
        grid_spec=pltpu.PrefetchScalarGridSpec(
            num_scalar_prefetch=2,
            grid=(1,),
            in_specs=[
                block((tok, packed)),
                block((2 * tok, packed)),
                block((2 * tok, packed)),
                block((head_count, tok)),
                block((2, head_count, tok)),
            ]
            + untouched(earlier),
            out_specs=[whole, whole, tall, tall],
        ),
        out_shape=[
            jax.ShapeDtypeStruct((head_count, size, size), f32),
            jax.ShapeDtypeStruct((head_count, size, size), f32),
            jax.ShapeDtypeStruct((head_count, tok, size), f32),
            jax.ShapeDtypeStruct((head_count, tok, size), f32),
        ],
        compiler_params=pltpu.CompilerParams(vmem_limit_bytes=16 << 20),
        name="local_terms",
    )(offset, resets, queries, keys, values, log_gate, beta, *earlier)


def vmem(count):
    return [pl.BlockSpec(memory_space=pltpu.VMEM)] * count


def untouched(earlier):
    return [pl.BlockSpec(memory_space=pl.ANY)] * len(earlier)


def step_kernel(choices, here_ref, *refs):
    maps, fills, state_ref, out_ref = refs[:choices], refs[choices:2 * choices], refs[2 * choices], refs[-1]
    here = here_ref[0]
    for n in range(choices):

        @pl.when(here == n)
        def _(n=n):
            for h in range(state_ref.shape[0]):
                out_ref[h] = dot3(maps[n][h], state_ref[h]) + fills[n][h]

    @pl.when(jnp.logical_or(here < 0, here >= choices))
    def _():
        out_ref[...] = fills[0][...]


def step(here, maps, fills, state, earlier=()):
    return pl.pallas_call(
        functools.partial(step_kernel, len(maps)),
        in_specs=[pl.BlockSpec(memory_space=pltpu.SMEM)]
        + vmem(2 * len(maps) + 1)
        + untouched(earlier),
        out_specs=pl.BlockSpec(memory_space=pltpu.VMEM),
        out_shape=jax.ShapeDtypeStruct(state.shape, f32),
        compiler_params=pltpu.CompilerParams(vmem_limit_bytes=8 << 20),
        cost_estimate=small_cost,
        name="state_step",
    )(here, *maps, *fills, state, *earlier)


def project_kernel(choices, groups, here_ref, place_ref, reach_ref, own_ref, *refs):
    states, w_ref = refs[:choices], refs[choices]
    keep_ref, head_ref, state_ref = refs[-3:]
    send_refs = refs[-3 - groups // 2:-3]
    heads, _, size = reach_ref.shape
    here, place = here_ref[0], place_ref[0]
    part = w_ref.shape[1] // groups

    @pl.when(here == 0)
    def _():
        for h in range(heads):
            head_ref[:, h * size:(h + 1) * size] = own_ref[h].astype(bf16)

    @pl.when(here > 0)
    def _():
        for n in range(choices):

            @pl.when(here == n + 1)
            def _(n=n):
                state_ref[...] = states[n][...]

        for h in range(heads):
            mixed = own_ref[h] + dot3(reach_ref[h], state_ref[h])
            head_ref[:, h * size:(h + 1) * size] = mixed.astype(bf16)

    for r in range(groups):
        start = pl.multiple_of((place ^ r) * part, part)
        share = mm(head_ref[...], w_ref[:, pl.ds(start, part)])
        if r % 2:
            send_refs[r // 2][...] = share
        else:
            keep_ref[r // 2] = share


def project(groups, here, place, reach, own, states, w_out, earlier=()):
    heads, tok, size = reach.shape
    part = w_out.shape[1] // groups
    mid = groups // 2
    smem = pl.BlockSpec(memory_space=pltpu.SMEM)
    outs = pl.pallas_call(
        functools.partial(project_kernel, len(states), groups),
        in_specs=[smem, smem] + vmem(3 + len(states)) + untouched(earlier),
        out_specs=vmem(mid + 1),
        out_shape=[jax.ShapeDtypeStruct((tok, part), f32)] * mid
        + [jax.ShapeDtypeStruct((mid, tok, part), f32)],
        scratch_shapes=[
            pltpu.VMEM((tok, heads * size), bf16),
            pltpu.VMEM((heads, size, size), f32),
        ],
        compiler_params=pltpu.CompilerParams(vmem_limit_bytes=16 << 20),
        cost_estimate=small_cost,
        name="project",
    )(here, place, reach, own, *states, w_out, *earlier)
    return outs[:mid], outs[mid]


def swapped(x, axis, bit):
    size = lax.axis_size(axis)
    return lax.ppermute(x, axis, [(i, i ^ bit) for i in range(size)])


def carry_on(devices, x, round_index, chunks):
    pairs = [(i, i + 1) for i in range(devices - 1) if 0 <= round_index - i < chunks]
    return lax.ppermute(x, "seq", pairs)


def add_kernel(mine_ref, *refs):
    leave_ref, stay_ref = refs[-2:]
    for r in range(mine_ref.shape[0]):
        out_ref = leave_ref if r % 2 else stay_ref
        out_ref[r // 2] = mine_ref[r] + refs[r][...]


def add_parts(mine, others, earlier=()):
    part = jax.ShapeDtypeStruct((mine.shape[0] // 2,) + mine.shape[1:], f32)
    return pl.pallas_call(
        add_kernel,
        in_specs=vmem(1 + len(others)) + untouched(earlier),
        out_specs=vmem(2),
        out_shape=[part] * 2,
        compiler_params=pltpu.CompilerParams(vmem_limit_bytes=4 << 20),
        cost_estimate=small_cost,
        name="add_parts",
    )(mine, *others, *earlier)


def reduced(send, keep):
    bit = 2
    while True:
        other = swapped(send, "head", bit)
        if keep.shape[0] == 1:
            return keep[0], other[0]
        send, keep = add_parts(keep, list(other))
        bit *= 2


def shards(queries, keys, values, log_gate, beta, resets, w_out):
    chunks, tok, packed = queries.shape
    groups = lax.axis_size("head")
    devices = lax.axis_size("seq")
    here = lax.axis_index("seq").astype(jnp.int32).reshape(1)
    offset = here * tok
    place = lax.axis_index("head").astype(jnp.int32).reshape(1)
    key_rows = keys.reshape(chunks, 2 * tok, packed)
    value_rows = values.reshape(chunks, 2 * tok, packed)

    def local(s, earlier=()):
        return local_terms(
            s, offset, resets, queries, key_rows, value_rows, log_gate, beta, earlier
        )

    if devices > 8:
        terms = [local(s) for s in range(chunks)]
        pairs = [(i, i + 1) for i in range(devices - 1)]
        no_choice = jnp.zeros((1,), jnp.int32)

        def turn(_, incoming):
            return tuple(
                lax.ppermute(
                    step(no_choice, [terms[s][0]], [terms[s][1]], incoming[s]), "seq", pairs
                )
                for s in range(chunks)
            )

        zero = tuple(jnp.zeros_like(terms[s][1]) for s in range(chunks))
        states = lax.fori_loop(0, devices - 1, turn, zero)
        outs = []
        for s in range(chunks):
            one = jnp.ones((1,), jnp.int32)
            sends, keep = project(groups, one, place, terms[s][2], terms[s][3], [states[s]], w_out)
            leave, stay = add_parts(keep, [swapped(x, "head", 1) for x in sends])
            outs.append(reduced(leave, stay))
        return jnp.stack([mine + other for mine, other in outs])

    last_round = chunks + devices - 3
    terms, arrived, partial, outs = [], [], [], []
    token = ()

    def add_up(c, token):
        sends, keep = partial[c]
        settled = (outs[c - 2][1],) if c == chunks - 1 and c >= 2 else ()
        leave, stay = add_parts(keep, [swapped(x, "head", 1) for x in sends], token + settled)
        outs.append(reduced(leave, stay))
        return (leave,)

    def projected(c, token):
        if 2 <= c < chunks - 1:
            token = token + (outs[c - 2][1],)
        partial.append(
            project(
                groups, here, place, terms[c][2], terms[c][3],
                [arrived[c + i] for i in range(devices - 1)], w_out, token,
            )
        )
        return (partial[c][1],)

    for r in range(last_round + 1):
        if r < chunks:
            terms.append(local(r, token))
            token = (terms[r][1],)
        if r == 0:
            sent = terms[0][1]
        else:
            valid = [r - i for i in range(devices - 1) if 0 <= r - i < chunks]
            sent = step(
                here - (r - valid[0]),
                [terms[c][0] for c in valid],
                [terms[c][1] for c in valid],
                arrived[r - 1],
                token,
            )
            token = (sent,)
        arrived.append(carry_on(devices, sent, r, chunks))
        done = r - devices + 1
        if done >= 1:
            token = add_up(done - 1, token)
        if done >= 0:
            token = projected(done, token)
    done = last_round - devices + 2
    token = projected(done, token)
    token = add_up(done - 1, token)
    token = add_up(done, token)
    return jnp.stack([mine + other for mine, other in outs])


def solution(mesh):
    placed = (
        P("grp", "seq", "head"),
        P("grp", "seq", None, "head"),
        P("grp", "seq", None, "head"),
        P("grp", "head", "seq"),
        P("grp", None, "head", "seq"),
        P("grp", None),
        P("head", None),
    )
    return jax.shard_map(
        shards, mesh=mesh, in_specs=placed, out_specs=P("grp", "seq", "head"), check_vma=False
    )
```

```python
import functools

import jax
import jax.numpy as jnp
from jax import lax
from jax.experimental import pallas as pl
from jax.experimental.pallas import tpu as pltpu
from jax.sharding import PartitionSpec as P

epsilon = 1e-06
small_cost = pl.CostEstimate(flops=1 << 20, transcendentals=0, bytes_accessed=1 << 10)
f32 = jnp.float32
bf16 = jnp.bfloat16


def mm(a, b):
    return lax.dot_general(a, b, (((1,), (0,)), ((), ())), preferred_element_type=f32)


def mm_nt(a, b):
    return lax.dot_general(a, b, (((1,), (1,)), ((), ())), preferred_element_type=f32)


def mm_tn(a, b):
    return lax.dot_general(a, b, (((0,), (0,)), ((), ())), preferred_element_type=f32)


def split(x):
    high = x.astype(bf16)
    return high, (x - high.astype(f32)).astype(bf16)


def split3(x):
    high, rest = x.astype(bf16), None
    rest = x - high.astype(f32)
    middle = rest.astype(bf16)
    return high, middle, (rest - middle.astype(f32)).astype(bf16)


def dot3(a, b):
    a_high, a_low = split(a)
    b_high, b_low = split(b)
    return mm(a_high, b_high) + (mm(a_low, b_high) + mm(a_high, b_low))


def iota(shape, axis):
    return lax.broadcasted_iota(jnp.int32, shape, axis)


def local_kernel(head_count, seq, offset_ref, resets_ref, q_ref, k_ref, v_ref, gate_ref, beta_ref,
                 *refs):
    transit_ref, filled_ref, reach_ref, own_ref = refs[-4:]
    tok = q_ref.shape[1]
    size = q_ref.shape[2] // head_count
    keys = 2 * tok
    half = keys // 2
    heads = range(head_count)
    offset = offset_ref[0]
    reset = [resets_ref[seq, i] for i in range(resets_ref.shape[1])]

    def doc_of(position):
        total = jnp.zeros_like(position)
        for r in reset:
            total = total + (r <= position).astype(jnp.int32)
        return total

    start_doc = sum(((r < offset).astype(jnp.int32) for r in reset), jnp.int32(0))
    last_doc = sum(((r <= offset + tok - 1).astype(jnp.int32) for r in reset), jnp.int32(0))
    doc_row = doc_of(offset + (iota((1, keys), 1) >> 1))
    doc_col = doc_of(offset + (iota((keys, 1), 0) >> 1))
    doc_tok = doc_of(offset + iota((tok, 1), 0))

    def stacked(x):
        return jnp.concatenate([p.astype(f32) for p in split3(x)], axis=0).astype(bf16)

    def folded(m):
        n = head_count
        return m[:n] + m[n:2 * n] + m[2 * n:3 * n]

    tok_i, key_i = iota((tok, keys), 0), iota((tok, keys), 1)
    gate3 = stacked(gate_ref[0])
    gs_row = folded(mm(gate3, (tok_i <= (key_i >> 1)).astype(f32).astype(bf16)))
    beta_row = folded(
        mm(stacked(beta_ref[0, 0]), (key_i == 2 * tok_i).astype(f32).astype(bf16))
        + mm(stacked(beta_ref[0, 1]), (key_i == 2 * tok_i + 1).astype(f32).astype(bf16))
    )
    gs_tok_row = folded(
        mm(gate3, (iota((tok, tok), 0) <= iota((tok, tok), 1)).astype(f32).astype(bf16))
    )
    gs_col, beta_col, gs_tok = gs_row.T, beta_row.T, gs_tok_row.T

    h_i, h_j = iota((half, half), 0), iota((half, half), 1)
    eye_half = h_i == h_j
    apart = jnp.where(h_i > h_j, h_i ^ h_j, 0)
    spans = [(1, 2)]
    while spans[-1][1] < half:
        spans.append((spans[-1][1], min(4 * spans[-1][1], half)))
    masks = [
        jnp.logical_and(apart >= a, apart < b).astype(f32).astype(bf16) for a, b in spans
    ]
    eye16 = eye_half.astype(f32).astype(bf16)
    eye_size = (iota((size, size), 0) == iota((size, size), 1)).astype(f32)
    top_mask = jnp.logical_and(h_i > h_j, doc_col[:half] == doc_row[:, :half])
    low_i, low_j = iota((half, keys), 0), iota((half, keys), 1)
    bottom_mask = jnp.logical_and(low_i + half > low_j, doc_col[half:] == doc_row)
    tok_linked = jnp.logical_and(
        (iota((tok, keys), 1) >> 1) <= iota((tok, keys), 0), doc_tok == doc_row
    )

    q = [q_ref[0, :, h * size:(h + 1) * size] for h in heads]
    k = [k_ref[0, :, :, h * size:(h + 1) * size].astype(f32).reshape(2 * tok, size).astype(bf16) for h in heads]
    v = [v_ref[0, :, :, h * size:(h + 1) * size].astype(f32).reshape(2 * tok, size).astype(bf16) for h in heads]

    def unit(x):
        return lax.rsqrt(jnp.sum(x * x, axis=1, keepdims=True) + epsilon)

    top, bottom, k_col, k_row, right = [], [], [], [], []
    for h in heads:
        gram_top = mm_nt(k[h][:half], k[h][:half])
        gram_bottom = mm_nt(k[h][half:], k[h])
        k32 = k[h].astype(f32)
        k_col.append(unit(k32))
        squares = jnp.concatenate(
            [
                jnp.sum(jnp.where(eye_half, g, 0.0), axis=0, keepdims=True)
                for g in (gram_top, gram_bottom[:, half:])
            ],
            axis=1,
        )
        k_row.append(lax.rsqrt(squares + epsilon))
        gr, gc = gs_row[h:h + 1], gs_col[:, h:h + 1]
        b_col = beta_col[:, h:h + 1]
        left = b_col * k_col[h]
        carried = jnp.where(doc_col == start_doc, jnp.exp(gc), 0.0)
        right.append(
            jnp.concatenate([k32 * (left * carried), v[h].astype(f32) * b_col], axis=1)
        )
        top.append(
            split(
                jnp.where(
                    top_mask,
                    gram_top * jnp.exp(gc[:half] - gr[:, :half]) * k_row[h][:, :half] * left[:half],
                    0.0,
                )
            )
        )
        bottom.append(
            split(
                jnp.where(
                    bottom_mask, gram_bottom * jnp.exp(gc[half:] - gr) * k_row[h] * left[half:], 0.0
                )
            )
        )

    blocks = [(h, b) for h in heads for b in range(2)]
    part = {(h, b): top[h][0] if b == 0 else bottom[h][0][:, half:] for h, b in blocks}
    inv = {key: eye16 - part[key] * masks[0] for key in blocks}
    for mask in masks[1:]:
        cross = {key: mm(inv[key], part[key] * mask).astype(bf16) for key in blocks}
        square = {key: mm(cross[key], cross[key]).astype(bf16) for key in blocks}
        near = {key: inv[key] - mm(cross[key], inv[key]).astype(bf16) for key in blocks}
        inv = {
            key: (near[key].astype(f32) + mm(square[key], near[key])).astype(bf16)
            for key in blocks
        }
    lower = []
    for h in heads:
        inner = mm(bottom[h][0][:, :half], inv[h, 0]).astype(bf16)
        lower.append(
            jnp.concatenate([-mm(inv[h, 1], inner).astype(bf16), inv[h, 1]], axis=1)
        )

    both = []
    for h in heads:
        rough = right[h].astype(bf16)
        g_top = mm(inv[h, 0], rough[:half]).astype(bf16)
        g_bottom = mm(lower[h], rough).astype(bf16)
        guess = jnp.concatenate([g_top, g_bottom], axis=0)
        rest_top = right[h][:half] - g_top.astype(f32) - (
            mm(top[h][0], g_top) + mm(top[h][1], g_top)
        )
        rest_bottom = right[h][half:] - g_bottom.astype(f32) - (
            mm(bottom[h][0], guess) + mm(bottom[h][1], guess)
        )
        rest = jnp.concatenate([rest_top.astype(bf16), rest_bottom.astype(bf16)], axis=0)
        both.append(
            jnp.concatenate(
                [
                    g_top.astype(f32) + mm(inv[h, 0], rest[:half]),
                    g_bottom.astype(f32) + mm(lower[h], rest),
                ],
                axis=0,
            )
        )

    for h in heads:
        gr, gc, gt = gs_row[h:h + 1], gs_col[:, h:h + 1], gs_tok[:, h:h + 1]
        last = gr[:, keys - 1:]
        carried_tok = jnp.where(doc_tok == start_doc, jnp.exp(gt), 0.0)
        closing = jnp.where(doc_col == last_doc, jnp.exp(last - gc), 0.0)
        end_high, end_low = split(both[h] * (closing * k_col[h]))
        ends = mm_tn(k[h], end_high) + mm_tn(k[h], end_low)
        keep = jnp.where(last_doc == start_doc, jnp.exp(last), 0.0)
        transit_ref[h] = keep * eye_size - ends[:, :size]
        filled_ref[h] = ends[:, size:]
        q32 = q[h].astype(f32)
        q_norm = unit(q32)
        probes = jnp.where(
            tok_linked, mm_nt(q[h], k[h]) * jnp.exp(gt - gr) * k_row[h] * q_norm, 0.0
        )
        outs = dot3(probes, both[h])
        reach_ref[h] = (carried_tok * q_norm) * q32 - outs[:, :size]
        own_ref[h] = outs[:, size:]


def local_terms(seq, offset, resets, queries, keys, values, log_gate, beta, earlier=()):
    _, tok, packed = queries.shape
    head_count = log_gate.shape[1]
    size = packed // head_count

    def block(shape):
        return pl.BlockSpec((1,) + shape, lambda i, o, r: (seq,) + (0,) * len(shape))

    whole = pl.BlockSpec((head_count, size, size), lambda i, o, r: (0, 0, 0))
    tall = pl.BlockSpec((head_count, tok, size), lambda i, o, r: (0, 0, 0))
    return pl.pallas_call(
        functools.partial(local_kernel, head_count, seq),
        grid_spec=pltpu.PrefetchScalarGridSpec(
            num_scalar_prefetch=2,
            grid=(1,),
            in_specs=[
                block((tok, packed)),
                block((tok, 2, packed)),
                block((tok, 2, packed)),
                block((head_count, tok)),
                block((2, head_count, tok)),
            ]
            + untouched(earlier),
            out_specs=[whole, whole, tall, tall],
        ),
        out_shape=[
            jax.ShapeDtypeStruct((head_count, size, size), f32),
            jax.ShapeDtypeStruct((head_count, size, size), f32),
            pltpu.HBM((head_count, tok, size), f32),
            pltpu.HBM((head_count, tok, size), f32),
        ],
        compiler_params=pltpu.CompilerParams(vmem_limit_bytes=16 << 20),
        name="local_terms",
    )(offset, resets, queries, keys, values, log_gate, beta, *earlier)


def vmem(count):
    return [pl.BlockSpec(memory_space=pltpu.VMEM)] * count


def untouched(earlier):
    return [pl.BlockSpec(memory_space=pl.ANY)] * len(earlier)


def step_kernel(choices, here_ref, *refs):
    maps, fills, state_ref, out_ref = refs[:choices], refs[choices:2 * choices], refs[2 * choices], refs[-1]
    here = here_ref[0]
    for n in range(choices):

        @pl.when(here == n)
        def _(n=n):
            for h in range(state_ref.shape[0]):
                out_ref[h] = dot3(maps[n][h], state_ref[h]) + fills[n][h]

    @pl.when(jnp.logical_or(here < 0, here >= choices))
    def _():
        out_ref[...] = fills[0][...]


def step(here, maps, fills, state, earlier=()):
    return pl.pallas_call(
        functools.partial(step_kernel, len(maps)),
        in_specs=[pl.BlockSpec(memory_space=pltpu.SMEM)]
        + vmem(2 * len(maps) + 1)
        + untouched(earlier),
        out_specs=pl.BlockSpec(memory_space=pltpu.VMEM),
        out_shape=jax.ShapeDtypeStruct(state.shape, f32),
        compiler_params=pltpu.CompilerParams(vmem_limit_bytes=8 << 20),
        cost_estimate=small_cost,
        name="state_step",
    )(here, *maps, *fills, state, *earlier)


def project_kernel(choices, groups, here_ref, place_ref, reach_ref, own_ref, *refs):
    states, w_ref = refs[:choices], refs[choices]
    keep_ref, head_ref, state_ref = refs[-3:]
    send_refs = refs[-3 - groups // 2:-3]
    heads, _, size = reach_ref.shape
    here, place = here_ref[0], place_ref[0]
    part = w_ref.shape[1] // groups

    @pl.when(here == 0)
    def _():
        for h in range(heads):
            head_ref[:, h * size:(h + 1) * size] = own_ref[h].astype(bf16)

    @pl.when(here > 0)
    def _():
        for n in range(choices):

            @pl.when(here == n + 1)
            def _(n=n):
                state_ref[...] = states[n][...]

        for h in range(heads):
            mixed = own_ref[h] + dot3(reach_ref[h], state_ref[h])
            head_ref[:, h * size:(h + 1) * size] = mixed.astype(bf16)

    for r in range(groups):
        start = pl.multiple_of((place ^ r) * part, part)
        share = mm(head_ref[...], w_ref[:, pl.ds(start, part)])
        if r % 2:
            send_refs[r // 2][...] = share
        else:
            keep_ref[r // 2] = share


def project(groups, here, place, reach, own, states, w_out, earlier=()):
    heads, tok, size = reach.shape
    part = w_out.shape[1] // groups
    mid = groups // 2
    smem = pl.BlockSpec(memory_space=pltpu.SMEM)
    outs = pl.pallas_call(
        functools.partial(project_kernel, len(states), groups),
        in_specs=[smem, smem] + vmem(3 + len(states)) + untouched(earlier),
        out_specs=vmem(mid + 1),
        out_shape=[jax.ShapeDtypeStruct((tok, part), f32)] * mid
        + [jax.ShapeDtypeStruct((mid, tok, part), f32)],
        scratch_shapes=[
            pltpu.VMEM((tok, heads * size), bf16),
            pltpu.VMEM((heads, size, size), f32),
        ],
        compiler_params=pltpu.CompilerParams(vmem_limit_bytes=16 << 20),
        cost_estimate=small_cost,
        name="project",
    )(here, place, reach, own, *states, w_out, *earlier)
    return outs[:mid], outs[mid]


def swapped(x, axis, bit):
    size = lax.axis_size(axis)
    return lax.ppermute(x, axis, [(i, i ^ bit) for i in range(size)])


def carry_on(devices, x, round_index, chunks):
    pairs = [(i, i + 1) for i in range(devices - 1) if 0 <= round_index - i < chunks]
    return lax.ppermute(x, "seq", pairs)


def add_kernel(mine_ref, *refs):
    leave_ref, stay_ref = refs[-2:]
    for r in range(mine_ref.shape[0]):
        out_ref = leave_ref if r % 2 else stay_ref
        out_ref[r // 2] = mine_ref[r] + refs[r][...]


def add_parts(mine, others, earlier=()):
    part = jax.ShapeDtypeStruct((mine.shape[0] // 2,) + mine.shape[1:], f32)
    return pl.pallas_call(
        add_kernel,
        in_specs=vmem(1 + len(others)) + untouched(earlier),
        out_specs=vmem(2),
        out_shape=[part] * 2,
        compiler_params=pltpu.CompilerParams(vmem_limit_bytes=4 << 20),
        cost_estimate=small_cost,
        name="add_parts",
    )(mine, *others, *earlier)


def reduced(send, keep):
    bit = 2
    while True:
        other = swapped(send, "head", bit)
        if keep.shape[0] == 1:
            return keep[0], other[0]
        send, keep = add_parts(keep, list(other))
        bit *= 2


def shards(queries, keys, values, log_gate, beta, resets, w_out):
    chunks, tok, packed = queries.shape
    groups = lax.axis_size("head")
    devices = lax.axis_size("seq")
    here = lax.axis_index("seq").astype(jnp.int32).reshape(1)
    offset = here * tok
    place = lax.axis_index("head").astype(jnp.int32).reshape(1)

    def local(s, earlier=()):
        return local_terms(
            s, offset, resets, queries, keys, values, log_gate, beta, earlier
        )

    if devices > 8:
        terms = [local(s) for s in range(chunks)]
        pairs = [(i, i + 1) for i in range(devices - 1)]
        no_choice = jnp.zeros((1,), jnp.int32)

        def turn(_, incoming):
            return tuple(
                lax.ppermute(
                    step(no_choice, [terms[s][0]], [terms[s][1]], incoming[s]), "seq", pairs
                )
                for s in range(chunks)
            )

        zero = tuple(jnp.zeros_like(terms[s][1]) for s in range(chunks))
        states = lax.fori_loop(0, devices - 1, turn, zero)
        outs = []
        for s in range(chunks):
            one = jnp.ones((1,), jnp.int32)
            sends, keep = project(groups, one, place, terms[s][2], terms[s][3], [states[s]], w_out)
            leave, stay = add_parts(keep, [swapped(x, "head", 1) for x in sends])
            outs.append(reduced(leave, stay))
        return jnp.stack([mine + other for mine, other in outs])

    last_round = chunks + devices - 3
    terms, arrived, partial, outs = [], [], [], []
    token = ()

    def add_up(c, token):
        sends, keep = partial[c]
        settled = (outs[c - 2][1],) if c == chunks - 1 and c >= 2 else ()
        leave, stay = add_parts(keep, [swapped(x, "head", 1) for x in sends], token + settled)
        outs.append(reduced(leave, stay))
        return (leave,)

    def projected(c, token):
        if 2 <= c < chunks - 1:
            token = token + (outs[c - 2][1],)
        partial.append(
            project(
                groups, here, place, terms[c][2], terms[c][3],
                [arrived[c + i] for i in range(devices - 1)], w_out, token,
            )
        )
        return (partial[c][1],)

    for r in range(last_round + 1):
        if r < chunks:
            terms.append(local(r, token))
            token = (terms[r][1],)
        if r == 0:
            sent = terms[0][1]
        else:
            valid = [r - i for i in range(devices - 1) if 0 <= r - i < chunks]
            sent = step(
                here - (r - valid[0]),
                [terms[c][0] for c in valid],
                [terms[c][1] for c in valid],
                arrived[r - 1],
                token,
            )
            token = (sent,)
        arrived.append(carry_on(devices, sent, r, chunks))
        done = r - devices + 1
        if done >= 1:
            token = add_up(done - 1, token)
        if done >= 0:
            token = projected(done, token)
    done = last_round - devices + 2
    token = projected(done, token)
    token = add_up(done - 1, token)
    token = add_up(done, token)
    return jnp.stack([mine + other for mine, other in outs])


def solution(mesh):
    placed = (
        P("grp", "seq", "head"),
        P("grp", "seq", None, "head"),
        P("grp", "seq", None, "head"),
        P("grp", "head", "seq"),
        P("grp", None, "head", "seq"),
        P("grp", None),
        P("head", None),
    )
    return jax.shard_map(
        shards, mesh=mesh, in_specs=placed, out_specs=P("grp", "seq", "head"), check_vma=False
    )
```

```python
import functools

import jax
import jax.numpy as jnp
from jax import lax
from jax.experimental import pallas as pl
from jax.experimental.pallas import tpu as pltpu
from jax.sharding import PartitionSpec as P

epsilon = 1e-06
small_cost = pl.CostEstimate(flops=1 << 20, transcendentals=0, bytes_accessed=1 << 10)
f32 = jnp.float32
bf16 = jnp.bfloat16


def mm(a, b):
    return lax.dot_general(a, b, (((1,), (0,)), ((), ())), preferred_element_type=f32)


def mm_nt(a, b):
    return lax.dot_general(a, b, (((1,), (1,)), ((), ())), preferred_element_type=f32)


def mm_tn(a, b):
    return lax.dot_general(a, b, (((0,), (0,)), ((), ())), preferred_element_type=f32)


def split(x):
    high = x.astype(bf16)
    return high, (x - high.astype(f32)).astype(bf16)


def split3(x):
    high, rest = x.astype(bf16), None
    rest = x - high.astype(f32)
    middle = rest.astype(bf16)
    return high, middle, (rest - middle.astype(f32)).astype(bf16)


def dot3(a, b):
    a_high, a_low = split(a)
    b_high, b_low = split(b)
    return mm(a_high, b_high) + (mm(a_low, b_high) + mm(a_high, b_low))


def iota(shape, axis):
    return lax.broadcasted_iota(jnp.int32, shape, axis)


def local_kernel(head_count, seq, fetch, ahead, later, offset_ref, resets_ref, *refs):
    refs = list(refs)
    inputs = [refs.pop(0) for _ in range(5)]
    sources = inputs if fetch else [refs.pop(0) for _ in range(5)] if ahead else []
    refs = refs[later:]
    transit_ref, filled_ref, reach_hbm, own_hbm = [refs.pop(0) for _ in range(4)]
    nexts = [refs.pop(0) for _ in range(5)] if ahead else []
    reach_ref, own_ref, sems = refs.pop(0), refs.pop(0), refs.pop(0)
    arrivals, ahead_copies = [], []
    if fetch:
        arrivals = [
            pltpu.make_async_copy(source.at[seq], refs[n], sems.at[n])
            for n, source in enumerate(sources)
        ]
        inputs = refs
    if ahead:
        ahead_copies = [
            pltpu.make_async_copy(source.at[seq + 1], nexts[n], sems.at[5 + n])
            for n, source in enumerate(sources)
        ]
    for copy in arrivals + ahead_copies:
        copy.start()
    q_ref, k_ref, v_ref, gate_ref, beta_ref = inputs
    tok = q_ref.shape[0]
    size = q_ref.shape[1] // head_count
    keys = 2 * tok
    half = keys // 2
    heads = range(head_count)
    offset = offset_ref[0]
    reset = [resets_ref[seq, i] for i in range(resets_ref.shape[1])]

    def doc_of(position):
        total = jnp.zeros_like(position)
        for r in reset:
            total = total + (r <= position).astype(jnp.int32)
        return total

    start_doc = sum(((r < offset).astype(jnp.int32) for r in reset), jnp.int32(0))
    last_doc = sum(((r <= offset + tok - 1).astype(jnp.int32) for r in reset), jnp.int32(0))
    doc_row = doc_of(offset + (iota((1, keys), 1) >> 1))
    doc_col = doc_of(offset + (iota((keys, 1), 0) >> 1))
    doc_tok = doc_of(offset + iota((tok, 1), 0))

    def stacked(x):
        return jnp.concatenate([p.astype(f32) for p in split3(x)], axis=0).astype(bf16)

    def folded(m):
        n = head_count
        return m[:n] + m[n:2 * n] + m[2 * n:3 * n]

    tok_i, key_i = iota((tok, keys), 0), iota((tok, keys), 1)
    for copy in arrivals:
        copy.wait()
    gate3 = stacked(gate_ref[...])
    gs_row = folded(mm(gate3, (tok_i <= (key_i >> 1)).astype(f32).astype(bf16)))
    beta_row = folded(
        mm(stacked(beta_ref[0]), (key_i == 2 * tok_i).astype(f32).astype(bf16))
        + mm(stacked(beta_ref[1]), (key_i == 2 * tok_i + 1).astype(f32).astype(bf16))
    )
    gs_tok_row = folded(
        mm(gate3, (iota((tok, tok), 0) <= iota((tok, tok), 1)).astype(f32).astype(bf16))
    )
    gs_col, beta_col, gs_tok = gs_row.T, beta_row.T, gs_tok_row.T

    h_i, h_j = iota((half, half), 0), iota((half, half), 1)
    eye_half = h_i == h_j
    apart = jnp.where(h_i > h_j, h_i ^ h_j, 0)
    spans = [(1, 2)]
    while spans[-1][1] < half:
        spans.append((spans[-1][1], min(4 * spans[-1][1], half)))
    masks = [
        jnp.logical_and(apart >= a, apart < b).astype(f32).astype(bf16) for a, b in spans
    ]
    eye16 = eye_half.astype(f32).astype(bf16)
    eye_size = (iota((size, size), 0) == iota((size, size), 1)).astype(f32)
    top_mask = jnp.logical_and(h_i > h_j, doc_col[:half] == doc_row[:, :half])
    low_i, low_j = iota((half, keys), 0), iota((half, keys), 1)
    bottom_mask = jnp.logical_and(low_i + half > low_j, doc_col[half:] == doc_row)
    tok_linked = jnp.logical_and(
        (iota((tok, keys), 1) >> 1) <= iota((tok, keys), 0), doc_tok == doc_row
    )

    q = [q_ref[:, h * size:(h + 1) * size] for h in heads]
    k = [k_ref[:, :, h * size:(h + 1) * size].astype(f32).reshape(2 * tok, size).astype(bf16) for h in heads]
    v = [v_ref[:, :, h * size:(h + 1) * size].astype(f32).reshape(2 * tok, size).astype(bf16) for h in heads]

    def unit(x):
        return lax.rsqrt(jnp.sum(x * x, axis=1, keepdims=True) + epsilon)

    top, bottom, k_col, k_row, right = [], [], [], [], []
    for h in heads:
        gram_top = mm_nt(k[h][:half], k[h][:half])
        gram_bottom = mm_nt(k[h][half:], k[h])
        k32 = k[h].astype(f32)
        k_col.append(unit(k32))
        squares = jnp.concatenate(
            [
                jnp.sum(jnp.where(eye_half, g, 0.0), axis=0, keepdims=True)
                for g in (gram_top, gram_bottom[:, half:])
            ],
            axis=1,
        )
        k_row.append(lax.rsqrt(squares + epsilon))
        gr, gc = gs_row[h:h + 1], gs_col[:, h:h + 1]
        b_col = beta_col[:, h:h + 1]
        left = b_col * k_col[h]
        carried = jnp.where(doc_col == start_doc, jnp.exp(gc), 0.0)
        right.append(
            jnp.concatenate([k32 * (left * carried), v[h].astype(f32) * b_col], axis=1)
        )
        top.append(
            split(
                jnp.where(
                    top_mask,
                    gram_top * jnp.exp(gc[:half] - gr[:, :half]) * k_row[h][:, :half] * left[:half],
                    0.0,
                )
            )
        )
        bottom.append(
            split(
                jnp.where(
                    bottom_mask, gram_bottom * jnp.exp(gc[half:] - gr) * k_row[h] * left[half:], 0.0
                )
            )
        )

    blocks = [(h, b) for h in heads for b in range(2)]
    part = {(h, b): top[h][0] if b == 0 else bottom[h][0][:, half:] for h, b in blocks}
    inv = {key: eye16 - part[key] * masks[0] for key in blocks}
    for mask in masks[1:]:
        cross = {key: mm(inv[key], part[key] * mask).astype(bf16) for key in blocks}
        square = {key: mm(cross[key], cross[key]).astype(bf16) for key in blocks}
        near = {key: inv[key] - mm(cross[key], inv[key]).astype(bf16) for key in blocks}
        inv = {
            key: (near[key].astype(f32) + mm(square[key], near[key])).astype(bf16)
            for key in blocks
        }
    lower = []
    for h in heads:
        inner = mm(bottom[h][0][:, :half], inv[h, 0]).astype(bf16)
        lower.append(
            jnp.concatenate([-mm(inv[h, 1], inner).astype(bf16), inv[h, 1]], axis=1)
        )

    both = []
    for h in heads:
        rough = right[h].astype(bf16)
        g_top = mm(inv[h, 0], rough[:half]).astype(bf16)
        g_bottom = mm(lower[h], rough).astype(bf16)
        guess = jnp.concatenate([g_top, g_bottom], axis=0)
        rest_top = right[h][:half] - g_top.astype(f32) - (
            mm(top[h][0], g_top) + mm(top[h][1], g_top)
        )
        rest_bottom = right[h][half:] - g_bottom.astype(f32) - (
            mm(bottom[h][0], guess) + mm(bottom[h][1], guess)
        )
        rest = jnp.concatenate([rest_top.astype(bf16), rest_bottom.astype(bf16)], axis=0)
        both.append(
            jnp.concatenate(
                [
                    g_top.astype(f32) + mm(inv[h, 0], rest[:half]),
                    g_bottom.astype(f32) + mm(lower[h], rest),
                ],
                axis=0,
            )
        )

    for h in heads:
        gr, gt = gs_row[h:h + 1], gs_tok[:, h:h + 1]
        carried_tok = jnp.where(doc_tok == start_doc, jnp.exp(gt), 0.0)
        q32 = q[h].astype(f32)
        q_norm = unit(q32)
        probes = jnp.where(
            tok_linked, mm_nt(q[h], k[h]) * jnp.exp(gt - gr) * k_row[h] * q_norm, 0.0
        )
        outs = dot3(probes, both[h])
        reach_ref[h] = (carried_tok * q_norm) * q32 - outs[:, :size]
        own_ref[h] = outs[:, size:]
    departures = [
        pltpu.make_async_copy(reach_ref, reach_hbm, sems.at[10]),
        pltpu.make_async_copy(own_ref, own_hbm, sems.at[11]),
    ]
    for copy in departures:
        copy.start()
    for h in heads:
        last = gs_row[h:h + 1, keys - 1:]
        closing = jnp.where(doc_col == last_doc, jnp.exp(last - gs_col[:, h:h + 1]), 0.0)
        end_high, end_low = split(both[h] * (closing * k_col[h]))
        ends = mm_tn(k[h], end_high) + mm_tn(k[h], end_low)
        keep = jnp.where(last_doc == start_doc, jnp.exp(last), 0.0)
        transit_ref[h] = keep * eye_size - ends[:, :size]
        filled_ref[h] = ends[:, size:]
    for copy in departures + ahead_copies:
        copy.wait()


def local_terms(seq, offset, resets, arrays, loaded, earlier=()):
    count, tok, packed = arrays[0].shape
    head_count = arrays[3].shape[1]
    size = packed // head_count
    fetch, ahead = loaded is None, seq + 1 < count
    smem, hbm = pl.BlockSpec(memory_space=pltpu.SMEM), pl.BlockSpec(memory_space=pltpu.HBM)
    operands = list(arrays) if fetch else list(loaded) + (list(arrays) if ahead else [])
    specs = [hbm] * 5 if fetch else vmem(5) + ([hbm] * 5 if ahead else [])
    squares = [pltpu.VMEM((head_count, size, size), f32)] * 2
    talls = [pltpu.HBM((head_count, tok, size), f32)] * 2
    blocks = [pltpu.VMEM(x.shape[1:], x.dtype) for x in arrays]
    outs = pl.pallas_call(
        functools.partial(local_kernel, head_count, seq, fetch, ahead, len(earlier)),
        in_specs=[smem, smem] + specs + untouched(earlier),
        out_specs=vmem(2) + [hbm] * 2 + (vmem(5) if ahead else []),
        out_shape=squares + talls + (blocks if ahead else []),
        scratch_shapes=[pltpu.VMEM((head_count, tok, size), f32)] * 2
        + [pltpu.SemaphoreType.DMA((12,))]
        + (blocks if fetch else []),
        compiler_params=pltpu.CompilerParams(vmem_limit_bytes=16 << 20),
        name="local_terms",
    )(offset, resets, *operands, *earlier)
    return outs[:4], outs[4:]


def vmem(count):
    return [pl.BlockSpec(memory_space=pltpu.VMEM)] * count


def untouched(earlier):
    return [pl.BlockSpec(memory_space=pl.ANY)] * len(earlier)


def step_kernel(choices, here_ref, *refs):
    maps, fills, state_ref, out_ref = refs[:choices], refs[choices:2 * choices], refs[2 * choices], refs[-1]
    here = here_ref[0]
    for n in range(choices):

        @pl.when(here == n)
        def _(n=n):
            for h in range(state_ref.shape[0]):
                out_ref[h] = dot3(maps[n][h], state_ref[h]) + fills[n][h]

    @pl.when(jnp.logical_or(here < 0, here >= choices))
    def _():
        out_ref[...] = fills[0][...]


def step(here, maps, fills, state, earlier=()):
    return pl.pallas_call(
        functools.partial(step_kernel, len(maps)),
        in_specs=[pl.BlockSpec(memory_space=pltpu.SMEM)]
        + vmem(2 * len(maps) + 1)
        + untouched(earlier),
        out_specs=pl.BlockSpec(memory_space=pltpu.VMEM),
        out_shape=pltpu.VMEM(state.shape, f32),
        compiler_params=pltpu.CompilerParams(vmem_limit_bytes=8 << 20),
        cost_estimate=small_cost,
        name="state_step",
    )(here, *maps, *fills, state, *earlier)


def project_kernel(choices, groups, here_ref, place_ref, reach_ref, own_ref, *refs):
    states, w_ref = refs[:choices], refs[choices]
    keep_ref, head_ref, state_ref = refs[-3:]
    send_refs = refs[-3 - groups // 2:-3]
    heads, _, size = reach_ref.shape
    here, place = here_ref[0], place_ref[0]
    part = w_ref.shape[1] // groups

    @pl.when(here == 0)
    def _():
        for h in range(heads):
            head_ref[:, h * size:(h + 1) * size] = own_ref[h].astype(bf16)

    @pl.when(here > 0)
    def _():
        for n in range(choices):

            @pl.when(here == n + 1)
            def _(n=n):
                state_ref[...] = states[n][...]

        for h in range(heads):
            mixed = own_ref[h] + dot3(reach_ref[h], state_ref[h])
            head_ref[:, h * size:(h + 1) * size] = mixed.astype(bf16)

    for r in range(groups):
        start = pl.multiple_of((place ^ r) * part, part)
        share = mm(head_ref[...], w_ref[:, pl.ds(start, part)])
        if r % 2:
            send_refs[r // 2][...] = share
        else:
            keep_ref[r // 2] = share


def project(groups, here, place, reach, own, states, w_out, earlier=()):
    heads, tok, size = reach.shape
    part = w_out.shape[1] // groups
    mid = groups // 2
    smem = pl.BlockSpec(memory_space=pltpu.SMEM)
    outs = pl.pallas_call(
        functools.partial(project_kernel, len(states), groups),
        in_specs=[smem, smem] + vmem(3 + len(states)) + untouched(earlier),
        out_specs=vmem(mid + 1),
        out_shape=[pltpu.VMEM((tok, part), f32)] * mid
        + [pltpu.VMEM((mid, tok, part), f32)],
        scratch_shapes=[
            pltpu.VMEM((tok, heads * size), bf16),
            pltpu.VMEM((heads, size, size), f32),
        ],
        compiler_params=pltpu.CompilerParams(vmem_limit_bytes=16 << 20),
        cost_estimate=small_cost,
        name="project",
    )(here, place, reach, own, *states, w_out, *earlier)
    return outs[:mid], outs[mid]


def swapped(x, axis, bit):
    size = lax.axis_size(axis)
    return lax.ppermute(x, axis, [(i, i ^ bit) for i in range(size)])


def carry_on(devices, x, round_index, chunks):
    pairs = [(i, i + 1) for i in range(devices - 1) if 0 <= round_index - i < chunks]
    return lax.ppermute(x, "seq", pairs)


def add_kernel(mine_ref, *refs):
    leave_ref, stay_ref = refs[-2:]
    for r in range(mine_ref.shape[0]):
        out_ref = leave_ref if r % 2 else stay_ref
        out_ref[r // 2] = mine_ref[r] + refs[r][...]


def add_parts(mine, others, earlier=()):
    part = pltpu.VMEM((mine.shape[0] // 2,) + mine.shape[1:], f32)
    return pl.pallas_call(
        add_kernel,
        in_specs=vmem(1 + len(others)) + untouched(earlier),
        out_specs=vmem(2),
        out_shape=[part] * 2,
        compiler_params=pltpu.CompilerParams(vmem_limit_bytes=4 << 20),
        cost_estimate=small_cost,
        name="add_parts",
    )(mine, *others, *earlier)


def reduced(send, keep):
    bit = 2
    while True:
        other = swapped(send, "head", bit)
        if keep.shape[0] == 1:
            return keep[0], other[0]
        send, keep = add_parts(keep, list(other))
        bit *= 2


def shards(queries, keys, values, log_gate, beta, resets, w_out):
    chunks, tok, packed = queries.shape
    groups = lax.axis_size("head")
    devices = lax.axis_size("seq")
    here = lax.axis_index("seq").astype(jnp.int32).reshape(1)
    offset = here * tok
    place = lax.axis_index("head").astype(jnp.int32).reshape(1)

    arrays = [
        pltpu.with_memory_space_constraint(x, pltpu.HBM)
        for x in (queries, keys, values, log_gate, beta)
    ]
    resets = pltpu.with_memory_space_constraint(resets, pltpu.HBM)
    loaded = None

    if devices > 8:
        terms = []
        for s in range(chunks):
            term, loaded = local_terms(s, offset, resets, arrays, loaded)
            terms.append(term)
        pairs = [(i, i + 1) for i in range(devices - 1)]
        no_choice = jnp.zeros((1,), jnp.int32)

        def turn(_, incoming):
            return tuple(
                lax.ppermute(
                    step(no_choice, [terms[s][0]], [terms[s][1]], incoming[s]), "seq", pairs
                )
                for s in range(chunks)
            )

        zero = tuple(jnp.zeros_like(terms[s][1]) for s in range(chunks))
        states = lax.fori_loop(0, devices - 1, turn, zero)
        outs = []
        for s in range(chunks):
            one = jnp.ones((1,), jnp.int32)
            sends, keep = project(groups, one, place, terms[s][2], terms[s][3], [states[s]], w_out)
            leave, stay = add_parts(keep, [swapped(x, "head", 1) for x in sends])
            outs.append(reduced(leave, stay))
        return jnp.stack([mine + other for mine, other in outs])

    last_round = chunks + devices - 3
    terms, arrived, partial, outs = [], [], [], []
    token = ()

    def add_up(c, token):
        sends, keep = partial[c]
        settled = (outs[c - 2][1],) if c == chunks - 1 and c >= 2 else ()
        leave, stay = add_parts(keep, [swapped(x, "head", 1) for x in sends], token + settled)
        outs.append(reduced(leave, stay))
        return (leave,)

    def projected(c, token):
        if 2 <= c < chunks - 1:
            token = token + (outs[c - 2][1],)
        partial.append(
            project(
                groups, here, place, terms[c][2], terms[c][3],
                [arrived[c + i] for i in range(devices - 1)], w_out, token,
            )
        )
        return (partial[c][1],)

    for r in range(last_round + 1):
        if r < chunks:
            term, loaded = local_terms(r, offset, resets, arrays, loaded, token)
            terms.append(term)
            token = (term[1],)
        if r == 0:
            sent = terms[0][1]
        else:
            valid = [r - i for i in range(devices - 1) if 0 <= r - i < chunks]
            sent = step(
                here - (r - valid[0]),
                [terms[c][0] for c in valid],
                [terms[c][1] for c in valid],
                arrived[r - 1],
                token,
            )
            token = (sent,)
        arrived.append(carry_on(devices, sent, r, chunks))
        done = r - devices + 1
        if done >= 1:
            token = add_up(done - 1, token)
        if done >= 0:
            token = projected(done, token)
    done = last_round - devices + 2
    token = projected(done, token)
    token = add_up(done - 1, token)
    token = add_up(done, token)
    return jnp.stack([mine + other for mine, other in outs])


def solution(mesh):
    placed = (
        P("grp", "seq", "head"),
        P("grp", "seq", None, "head"),
        P("grp", "seq", None, "head"),
        P("grp", "head", "seq"),
        P("grp", None, "head", "seq"),
        P("grp", None),
        P("head", None),
    )
    return jax.shard_map(
        shards, mesh=mesh, in_specs=placed, out_specs=P("grp", "seq", "head"), check_vma=False
    )
```

```python
import functools

import jax
import jax.numpy as jnp
from jax import lax
from jax.experimental import pallas as pl
from jax.experimental.pallas import tpu as pltpu
from jax.sharding import PartitionSpec as P

epsilon = 1e-06
log2_e = 1.4426950408889634
small_cost = pl.CostEstimate(flops=1 << 20, transcendentals=0, bytes_accessed=1 << 10)
f32 = jnp.float32
bf16 = jnp.bfloat16


def mm(a, b):
    return lax.dot_general(a, b, (((1,), (0,)), ((), ())), preferred_element_type=f32)


def mm_nt(a, b):
    return lax.dot_general(a, b, (((1,), (1,)), ((), ())), preferred_element_type=f32)


def mm_tn(a, b):
    return lax.dot_general(a, b, (((0,), (0,)), ((), ())), preferred_element_type=f32)


def split(x):
    high = x.astype(bf16)
    return high, (x - high.astype(f32)).astype(bf16)


def split3(x):
    high, rest = x.astype(bf16), None
    rest = x - high.astype(f32)
    middle = rest.astype(bf16)
    return high, middle, (rest - middle.astype(f32)).astype(bf16)


def dot3(a, b):
    a_high, a_low = split(a)
    b_high, b_low = split(b)
    return mm(a_high, b_high) + (mm(a_low, b_high) + mm(a_high, b_low))


def iota(shape, axis):
    return lax.broadcasted_iota(jnp.int32, shape, axis)


def local_kernel(head_count, seq, fetch, ahead, later, offset_ref, resets_ref, *refs):
    refs = list(refs)
    inputs = [refs.pop(0) for _ in range(5)]
    sources = inputs if fetch else [refs.pop(0) for _ in range(5)] if ahead else []
    refs = refs[later:]
    transit_ref, filled_ref, reach_hbm, own_hbm = [refs.pop(0) for _ in range(4)]
    nexts = [refs.pop(0) for _ in range(5)] if ahead else []
    reach_ref, own_ref, sems = refs.pop(0), refs.pop(0), refs.pop(0)
    arrivals, ahead_copies = [], []
    if fetch:
        arrivals = [
            pltpu.make_async_copy(source.at[seq], refs[n], sems.at[n])
            for n, source in enumerate(sources)
        ]
        inputs = refs
    if ahead:
        ahead_copies = [
            pltpu.make_async_copy(source.at[seq + 1], nexts[n], sems.at[5 + n])
            for n, source in enumerate(sources)
        ]
    for copy in arrivals + ahead_copies:
        copy.start()
    q_ref, k_ref, v_ref, gate_ref, beta_ref = inputs
    tok = q_ref.shape[0]
    size = q_ref.shape[1] // head_count
    keys = 2 * tok
    half = keys // 2
    heads = range(head_count)
    offset = offset_ref[0]
    reset = [resets_ref[seq, i] for i in range(resets_ref.shape[1])]

    def doc_of(position):
        total = jnp.zeros_like(position)
        for r in reset:
            total = total + (r <= position).astype(jnp.int32)
        return total

    start_doc = sum(((r < offset).astype(jnp.int32) for r in reset), jnp.int32(0))
    last_doc = sum(((r <= offset + tok - 1).astype(jnp.int32) for r in reset), jnp.int32(0))
    doc_row = doc_of(offset + (iota((1, keys), 1) >> 1))
    doc_col = doc_of(offset + (iota((keys, 1), 0) >> 1))
    doc_tok = doc_of(offset + iota((tok, 1), 0))

    def stacked(x):
        return jnp.concatenate([p.astype(f32) for p in split3(x)], axis=0).astype(bf16)

    def folded(m):
        n = head_count
        return m[:n] + m[n:2 * n] + m[2 * n:3 * n]

    tok_i, key_i = iota((tok, keys), 0), iota((tok, keys), 1)
    for copy in arrivals:
        copy.wait()
    gate3 = stacked(gate_ref[...])
    gs_row = log2_e * folded(mm(gate3, (tok_i <= (key_i >> 1)).astype(f32).astype(bf16)))
    beta_row = folded(
        mm(stacked(beta_ref[0]), (key_i == 2 * tok_i).astype(f32).astype(bf16))
        + mm(stacked(beta_ref[1]), (key_i == 2 * tok_i + 1).astype(f32).astype(bf16))
    )
    gs_tok_row = log2_e * folded(
        mm(gate3, (iota((tok, tok), 0) <= iota((tok, tok), 1)).astype(f32).astype(bf16))
    )
    gs_col, beta_col, gs_tok = gs_row.T, beta_row.T, gs_tok_row.T

    h_i, h_j = iota((half, half), 0), iota((half, half), 1)
    eye_half = h_i == h_j
    apart = jnp.where(h_i > h_j, h_i ^ h_j, 0)
    spans = [(1, 2)]
    while spans[-1][1] < half:
        spans.append((spans[-1][1], min(4 * spans[-1][1], half)))
    masks = [
        jnp.logical_and(apart >= a, apart < b).astype(f32).astype(bf16) for a, b in spans
    ]
    eye16 = eye_half.astype(f32).astype(bf16)
    eye_size = (iota((size, size), 0) == iota((size, size), 1)).astype(f32)
    top_mask = jnp.logical_and(h_i > h_j, doc_col[:half] == doc_row[:, :half])
    low_i, low_j = iota((half, keys), 0), iota((half, keys), 1)
    bottom_mask = jnp.logical_and(low_i + half > low_j, doc_col[half:] == doc_row)
    tok_linked = jnp.logical_and(
        (iota((tok, keys), 1) >> 1) <= iota((tok, keys), 0), doc_tok == doc_row
    )

    q = [q_ref[:, h * size:(h + 1) * size] for h in heads]
    k = [k_ref[:, :, h * size:(h + 1) * size].astype(f32).reshape(2 * tok, size).astype(bf16) for h in heads]
    v = [v_ref[:, :, h * size:(h + 1) * size].astype(f32).reshape(2 * tok, size).astype(bf16) for h in heads]

    def unit(x):
        return lax.rsqrt(jnp.sum(x * x, axis=1, keepdims=True) + epsilon)

    gram_top = [mm_nt(k[h][:half], k[h][:half]) for h in heads]
    gram_bottom = [mm_nt(k[h][half:], k[h]) for h in heads]
    squares = [
        jnp.concatenate(
            [
                jnp.sum(jnp.where(eye_half, g, 0.0), axis=0, keepdims=True)
                for g in (gram_top[h], gram_bottom[h][:, half:])
            ],
            axis=1,
        )
        for h in heads
    ]
    k_row = lax.rsqrt(jnp.concatenate(squares, axis=0) + epsilon)
    k_col = k_row.T
    left = beta_col * k_col
    carried = left * jnp.where(doc_col == start_doc, jnp.exp2(gs_col), 0.0)
    closing = k_col * jnp.where(doc_col == last_doc, jnp.exp2(gs_col[keys - 1:] - gs_col), 0.0)
    one_top = eye_half.astype(f32)
    one_bottom = jnp.concatenate([jnp.zeros((half, half), f32), one_top], axis=1)
    top, bottom, right = [], [], []
    for h in heads:
        gr, gc = gs_row[h:h + 1], gs_col[:, h:h + 1]
        kr, lc = k_row[h:h + 1], left[:, h:h + 1]
        right.append(
            jnp.concatenate(
                [
                    k[h].astype(f32) * carried[:, h:h + 1],
                    v[h].astype(f32) * beta_col[:, h:h + 1],
                ],
                axis=1,
            )
        )
        top.append(
            split(
                jnp.where(
                    top_mask,
                    gram_top[h] * jnp.exp2(gc[:half] - gr[:, :half]) * kr[:, :half] * lc[:half],
                    one_top,
                )
            )
        )
        bottom.append(
            split(
                jnp.where(
                    bottom_mask,
                    gram_bottom[h] * jnp.exp2(gc[half:] - gr) * kr * lc[half:],
                    one_bottom,
                )
            )
        )

    blocks = [(h, b) for h in heads for b in range(2)]
    part = {(h, b): top[h][0] if b == 0 else bottom[h][0][:, half:] for h, b in blocks}
    inv = {key: eye16 - part[key] * masks[0] for key in blocks}
    for mask in masks[1:]:
        cross = {key: mm(inv[key], part[key] * mask).astype(bf16) for key in blocks}
        square = {key: mm(cross[key], cross[key]).astype(bf16) for key in blocks}
        near = {key: inv[key] - mm(cross[key], inv[key]).astype(bf16) for key in blocks}
        inv = {
            key: (near[key].astype(f32) + mm(square[key], near[key])).astype(bf16)
            for key in blocks
        }
    lower = []
    for h in heads:
        inner = mm(bottom[h][0][:, :half], inv[h, 0]).astype(bf16)
        lower.append(
            jnp.concatenate([-mm(inv[h, 1], inner).astype(bf16), inv[h, 1]], axis=1)
        )

    both = []
    for h in heads:
        rough = right[h].astype(bf16)
        g_top = mm(inv[h, 0], rough[:half]).astype(bf16)
        g_bottom = mm(lower[h], rough).astype(bf16)
        rest_top = right[h][:half] - mm(
            jnp.concatenate(top[h], axis=1), jnp.concatenate([g_top, g_top], axis=0)
        )
        rest_bottom = right[h][half:] - mm(
            jnp.concatenate(bottom[h], axis=1),
            jnp.concatenate([g_top, g_bottom, g_top, g_bottom], axis=0),
        )
        rest_top, rest_bottom = rest_top.astype(bf16), rest_bottom.astype(bf16)
        both.append(
            jnp.concatenate(
                [
                    mm(
                        jnp.concatenate([inv[h, 0], eye16], axis=1),
                        jnp.concatenate([rest_top, g_top], axis=0),
                    ),
                    mm(
                        jnp.concatenate([lower[h], eye16], axis=1),
                        jnp.concatenate([rest_top, rest_bottom, g_bottom], axis=0),
                    ),
                ],
                axis=0,
            )
        )

    carried_tok = jnp.where(doc_tok == start_doc, jnp.exp2(gs_tok), 0.0)
    for h in heads:
        gr, gt = gs_row[h:h + 1], gs_tok[:, h:h + 1]
        q32 = q[h].astype(f32)
        q_norm = unit(q32)
        probes = jnp.where(
            tok_linked, mm_nt(q[h], k[h]) * jnp.exp2(gt - gr) * k_row[h:h + 1] * q_norm, 0.0
        )
        outs = dot3(probes, both[h])
        reach_ref[h] = (carried_tok[:, h:h + 1] * q_norm) * q32 - outs[:, :size]
        own_ref[h] = outs[:, size:]
    departures = [
        pltpu.make_async_copy(reach_ref, reach_hbm, sems.at[10]),
        pltpu.make_async_copy(own_ref, own_hbm, sems.at[11]),
    ]
    for copy in departures:
        copy.start()
    for h in heads:
        end_high, end_low = split(both[h] * closing[:, h:h + 1])
        ends = mm_tn(k[h], end_high) + mm_tn(k[h], end_low)
        keep = jnp.where(last_doc == start_doc, jnp.exp2(gs_row[h:h + 1, keys - 1:]), 0.0)
        transit_ref[h] = keep * eye_size - ends[:, :size]
        filled_ref[h] = ends[:, size:]
    for copy in departures + ahead_copies:
        copy.wait()


def local_terms(seq, offset, resets, arrays, loaded, earlier=()):
    count, tok, packed = arrays[0].shape
    head_count = arrays[3].shape[1]
    size = packed // head_count
    fetch, ahead = loaded is None, seq + 1 < count
    smem, hbm = pl.BlockSpec(memory_space=pltpu.SMEM), pl.BlockSpec(memory_space=pltpu.HBM)
    operands = list(arrays) if fetch else list(loaded) + (list(arrays) if ahead else [])
    specs = [hbm] * 5 if fetch else vmem(5) + ([hbm] * 5 if ahead else [])
    squares = [pltpu.VMEM((head_count, size, size), f32)] * 2
    talls = [pltpu.HBM((head_count, tok, size), f32)] * 2
    blocks = [pltpu.VMEM(x.shape[1:], x.dtype) for x in arrays]
    outs = pl.pallas_call(
        functools.partial(local_kernel, head_count, seq, fetch, ahead, len(earlier)),
        in_specs=[smem, smem] + specs + untouched(earlier),
        out_specs=vmem(2) + [hbm] * 2 + (vmem(5) if ahead else []),
        out_shape=squares + talls + (blocks if ahead else []),
        scratch_shapes=[pltpu.VMEM((head_count, tok, size), f32)] * 2
        + [pltpu.SemaphoreType.DMA((12,))]
        + (blocks if fetch else []),
        compiler_params=pltpu.CompilerParams(vmem_limit_bytes=16 << 20),
        name="local_terms",
    )(offset, resets, *operands, *earlier)
    return outs[:4], outs[4:]


def vmem(count):
    return [pl.BlockSpec(memory_space=pltpu.VMEM)] * count


def untouched(earlier):
    return [pl.BlockSpec(memory_space=pl.ANY)] * len(earlier)


def step_kernel(choices, here_ref, *refs):
    maps, fills, state_ref, out_ref = refs[:choices], refs[choices:2 * choices], refs[2 * choices], refs[-1]
    here = here_ref[0]
    for n in range(choices):

        @pl.when(here == n)
        def _(n=n):
            for h in range(state_ref.shape[0]):
                out_ref[h] = dot3(maps[n][h], state_ref[h]) + fills[n][h]

    @pl.when(jnp.logical_or(here < 0, here >= choices))
    def _():
        out_ref[...] = fills[0][...]


def step(here, maps, fills, state, earlier=()):
    return pl.pallas_call(
        functools.partial(step_kernel, len(maps)),
        in_specs=[pl.BlockSpec(memory_space=pltpu.SMEM)]
        + vmem(2 * len(maps) + 1)
        + untouched(earlier),
        out_specs=pl.BlockSpec(memory_space=pltpu.VMEM),
        out_shape=pltpu.VMEM(state.shape, f32),
        compiler_params=pltpu.CompilerParams(vmem_limit_bytes=8 << 20),
        cost_estimate=small_cost,
        name="state_step",
    )(here, *maps, *fills, state, *earlier)


def project_kernel(choices, groups, here_ref, place_ref, reach_ref, own_ref, *refs):
    states, w_ref = refs[:choices], refs[choices]
    keep_ref, head_ref, state_ref = refs[-3:]
    send_refs = refs[-3 - groups // 2:-3]
    heads, _, size = reach_ref.shape
    here, place = here_ref[0], place_ref[0]
    part = w_ref.shape[1] // groups

    @pl.when(here == 0)
    def _():
        for h in range(heads):
            head_ref[:, h * size:(h + 1) * size] = own_ref[h].astype(bf16)

    @pl.when(here > 0)
    def _():
        for n in range(choices):

            @pl.when(here == n + 1)
            def _(n=n):
                state_ref[...] = states[n][...]

        for h in range(heads):
            mixed = own_ref[h] + dot3(reach_ref[h], state_ref[h])
            head_ref[:, h * size:(h + 1) * size] = mixed.astype(bf16)

    for r in range(groups):
        start = pl.multiple_of((place ^ r) * part, part)
        share = mm(head_ref[...], w_ref[:, pl.ds(start, part)])
        if r % 2:
            send_refs[r // 2][...] = share
        else:
            keep_ref[r // 2] = share


def project(groups, here, place, reach, own, states, w_out, earlier=()):
    heads, tok, size = reach.shape
    part = w_out.shape[1] // groups
    mid = groups // 2
    smem = pl.BlockSpec(memory_space=pltpu.SMEM)
    outs = pl.pallas_call(
        functools.partial(project_kernel, len(states), groups),
        in_specs=[smem, smem] + vmem(3 + len(states)) + untouched(earlier),
        out_specs=vmem(mid + 1),
        out_shape=[pltpu.VMEM((tok, part), f32)] * mid
        + [pltpu.VMEM((mid, tok, part), f32)],
        scratch_shapes=[
            pltpu.VMEM((tok, heads * size), bf16),
            pltpu.VMEM((heads, size, size), f32),
        ],
        compiler_params=pltpu.CompilerParams(vmem_limit_bytes=16 << 20),
        cost_estimate=small_cost,
        name="project",
    )(here, place, reach, own, *states, w_out, *earlier)
    return outs[:mid], outs[mid]


def swapped(x, axis, bit):
    size = lax.axis_size(axis)
    return lax.ppermute(x, axis, [(i, i ^ bit) for i in range(size)])


def carry_on(devices, x, round_index, chunks):
    pairs = [(i, i + 1) for i in range(devices - 1) if 0 <= round_index - i < chunks]
    return lax.ppermute(x, "seq", pairs)


def add_kernel(mine_ref, *refs):
    leave_ref, stay_ref = refs[-2:]
    for r in range(mine_ref.shape[0]):
        out_ref = leave_ref if r % 2 else stay_ref
        out_ref[r // 2] = mine_ref[r] + refs[r][...]


def add_parts(mine, others, earlier=()):
    part = pltpu.VMEM((mine.shape[0] // 2,) + mine.shape[1:], f32)
    return pl.pallas_call(
        add_kernel,
        in_specs=vmem(1 + len(others)) + untouched(earlier),
        out_specs=vmem(2),
        out_shape=[part] * 2,
        compiler_params=pltpu.CompilerParams(vmem_limit_bytes=4 << 20),
        cost_estimate=small_cost,
        name="add_parts",
    )(mine, *others, *earlier)


def reduced(send, keep):
    bit = 2
    while True:
        other = swapped(send, "head", bit)
        if keep.shape[0] == 1:
            return keep[0], other[0]
        send, keep = add_parts(keep, list(other))
        bit *= 2


def shards(queries, keys, values, log_gate, beta, resets, w_out):
    chunks, tok, packed = queries.shape
    groups = lax.axis_size("head")
    devices = lax.axis_size("seq")
    here = lax.axis_index("seq").astype(jnp.int32).reshape(1)
    offset = here * tok
    place = lax.axis_index("head").astype(jnp.int32).reshape(1)

    arrays = [
        pltpu.with_memory_space_constraint(x, pltpu.HBM)
        for x in (queries, keys, values, log_gate, beta)
    ]
    resets = pltpu.with_memory_space_constraint(resets, pltpu.HBM)
    loaded = None

    if devices > 8:
        terms = []
        for s in range(chunks):
            term, loaded = local_terms(s, offset, resets, arrays, loaded)
            terms.append(term)
        pairs = [(i, i + 1) for i in range(devices - 1)]
        no_choice = jnp.zeros((1,), jnp.int32)

        def turn(_, incoming):
            return tuple(
                lax.ppermute(
                    step(no_choice, [terms[s][0]], [terms[s][1]], incoming[s]), "seq", pairs
                )
                for s in range(chunks)
            )

        zero = tuple(jnp.zeros_like(terms[s][1]) for s in range(chunks))
        states = lax.fori_loop(0, devices - 1, turn, zero)
        outs = []
        for s in range(chunks):
            one = jnp.ones((1,), jnp.int32)
            sends, keep = project(groups, one, place, terms[s][2], terms[s][3], [states[s]], w_out)
            leave, stay = add_parts(keep, [swapped(x, "head", 1) for x in sends])
            outs.append(reduced(leave, stay))
        return jnp.stack([mine + other for mine, other in outs])

    last_round = chunks + devices - 3
    terms, arrived, partial, outs = [], [], [], []
    token = ()

    def add_up(c, token):
        sends, keep = partial[c]
        settled = (outs[c - 2][1],) if c == chunks - 1 and c >= 2 else ()
        leave, stay = add_parts(keep, [swapped(x, "head", 1) for x in sends], token + settled)
        outs.append(reduced(leave, stay))
        return (leave,)

    def projected(c, token):
        if 2 <= c < chunks - 1:
            token = token + (outs[c - 2][1],)
        partial.append(
            project(
                groups, here, place, terms[c][2], terms[c][3],
                [arrived[c + i] for i in range(devices - 1)], w_out, token,
            )
        )
        return (partial[c][1],)

    for r in range(last_round + 1):
        if r < chunks:
            term, loaded = local_terms(r, offset, resets, arrays, loaded, token)
            terms.append(term)
            token = (term[1],)
        if r == 0:
            sent = terms[0][1]
        else:
            valid = [r - i for i in range(devices - 1) if 0 <= r - i < chunks]
            sent = step(
                here - (r - valid[0]),
                [terms[c][0] for c in valid],
                [terms[c][1] for c in valid],
                arrived[r - 1],
                token,
            )
            token = (sent,)
        arrived.append(carry_on(devices, sent, r, chunks))
        done = r - devices + 1
        if done >= 1:
            token = add_up(done - 1, token)
        if done >= 0:
            token = projected(done, token)
    done = last_round - devices + 2
    token = projected(done, token)
    token = add_up(done - 1, token)
    token = add_up(done, token)
    return jnp.stack([mine + other for mine, other in outs])


def solution(mesh):
    placed = (
        P("grp", "seq", "head"),
        P("grp", "seq", None, "head"),
        P("grp", "seq", None, "head"),
        P("grp", "head", "seq"),
        P("grp", None, "head", "seq"),
        P("grp", None),
        P("head", None),
    )
    return jax.shard_map(
        shards, mesh=mesh, in_specs=placed, out_specs=P("grp", "seq", "head"), check_vma=False
    )
```

```python
import functools

import jax
import jax.numpy as jnp
from jax import lax
from jax.experimental import pallas as pl
from jax.experimental.pallas import tpu as pltpu
from jax.sharding import PartitionSpec as P

epsilon = 1e-06
log2_e = 1.4426950408889634
small_cost = pl.CostEstimate(flops=1 << 20, transcendentals=0, bytes_accessed=1 << 10)
f32 = jnp.float32
bf16 = jnp.bfloat16


def mm(a, b):
    return lax.dot_general(a, b, (((1,), (0,)), ((), ())), preferred_element_type=f32)


def mm_nt(a, b):
    return lax.dot_general(a, b, (((1,), (1,)), ((), ())), preferred_element_type=f32)


def mm_tn(a, b):
    return lax.dot_general(a, b, (((0,), (0,)), ((), ())), preferred_element_type=f32)


def split(x):
    high = x.astype(bf16)
    return high, (x - high.astype(f32)).astype(bf16)


def split3(x):
    high, rest = x.astype(bf16), None
    rest = x - high.astype(f32)
    middle = rest.astype(bf16)
    return high, middle, (rest - middle.astype(f32)).astype(bf16)


def dot3(a, b):
    a_high, a_low = split(a)
    b_high, b_low = split(b)
    return mm(a_high, b_high) + (mm(a_low, b_high) + mm(a_high, b_low))


def iota(shape, axis):
    return lax.broadcasted_iota(jnp.int32, shape, axis)


def local_kernel(head_count, seq, fetch, ahead, later, offset_ref, resets_ref, *refs):
    refs = list(refs)
    inputs = [refs.pop(0) for _ in range(5)]
    sources = inputs if fetch else [refs.pop(0) for _ in range(5)] if ahead else []
    refs = refs[later:]
    transit_ref, filled_ref, reach_hbm, own_hbm = [refs.pop(0) for _ in range(4)]
    nexts = [refs.pop(0) for _ in range(5)] if ahead else []
    reach_ref, own_ref, sems = refs.pop(0), refs.pop(0), refs.pop(0)
    arrivals, ahead_copies = [], []
    if fetch:
        arrivals = [
            pltpu.make_async_copy(source.at[seq], refs[n], sems.at[n])
            for n, source in enumerate(sources)
        ]
        inputs = refs
    if ahead:
        ahead_copies = [
            pltpu.make_async_copy(source.at[seq + 1], nexts[n], sems.at[5 + n])
            for n, source in enumerate(sources)
        ]
    for copy in arrivals + ahead_copies:
        copy.start()
    q_ref, k_ref, v_ref, gate_ref, beta_ref = inputs
    tok = q_ref.shape[0]
    size = q_ref.shape[1] // head_count
    keys = 2 * tok
    half = keys // 2
    heads = range(head_count)
    offset = offset_ref[0]
    reset = [resets_ref[seq, i] for i in range(resets_ref.shape[1])]

    def doc_of(position):
        total = jnp.zeros_like(position)
        for r in reset:
            total = total + (r <= position).astype(jnp.int32)
        return total

    start_doc = sum(((r < offset).astype(jnp.int32) for r in reset), jnp.int32(0))
    last_doc = sum(((r <= offset + tok - 1).astype(jnp.int32) for r in reset), jnp.int32(0))
    doc_row = doc_of(offset + (iota((1, keys), 1) >> 1))
    doc_col = doc_of(offset + (iota((keys, 1), 0) >> 1))
    doc_tok = doc_of(offset + iota((tok, 1), 0))

    def stacked(x):
        return jnp.concatenate([p.astype(f32) for p in split3(x)], axis=0).astype(bf16)

    def folded(m):
        n = head_count
        return m[:n] + m[n:2 * n] + m[2 * n:3 * n]

    tok_i, key_i = iota((tok, keys), 0), iota((tok, keys), 1)
    for copy in arrivals:
        copy.wait()
    gate3 = stacked(gate_ref[...])
    gs_row = log2_e * folded(mm(gate3, (tok_i <= (key_i >> 1)).astype(f32).astype(bf16)))
    beta_row = folded(
        mm(stacked(beta_ref[0]), (key_i == 2 * tok_i).astype(f32).astype(bf16))
        + mm(stacked(beta_ref[1]), (key_i == 2 * tok_i + 1).astype(f32).astype(bf16))
    )
    gs_tok_row = log2_e * folded(
        mm(gate3, (iota((tok, tok), 0) <= iota((tok, tok), 1)).astype(f32).astype(bf16))
    )
    gs_col, beta_col, gs_tok = gs_row.T, beta_row.T, gs_tok_row.T

    h_i, h_j = iota((half, half), 0), iota((half, half), 1)
    eye_half = h_i == h_j
    apart = jnp.where(h_i > h_j, h_i ^ h_j, 0)
    spans = [(1, 2)]
    while spans[-1][1] < half:
        spans.append((spans[-1][1], min(4 * spans[-1][1], half)))
    masks = [
        jnp.logical_and(apart >= a, apart < b).astype(f32).astype(bf16) for a, b in spans
    ]
    eye16 = eye_half.astype(f32).astype(bf16)
    eye_size = (iota((size, size), 0) == iota((size, size), 1)).astype(f32)
    top_mask = jnp.logical_and(h_i > h_j, doc_col[:half] == doc_row[:, :half])
    low_i, low_j = iota((half, keys), 0), iota((half, keys), 1)
    bottom_mask = jnp.logical_and(low_i + half > low_j, doc_col[half:] == doc_row)
    tok_linked = jnp.logical_and(
        (iota((tok, keys), 1) >> 1) <= iota((tok, keys), 0), doc_tok == doc_row
    )

    q = [q_ref[:, h * size:(h + 1) * size] for h in heads]
    k = [k_ref[:, :, h * size:(h + 1) * size].astype(f32).reshape(2 * tok, size).astype(bf16) for h in heads]
    v = [v_ref[:, :, h * size:(h + 1) * size].astype(f32).reshape(2 * tok, size).astype(bf16) for h in heads]

    def unit(x):
        return lax.rsqrt(jnp.sum(x * x, axis=1, keepdims=True) + epsilon)

    gram_top = [mm_nt(k[h][:half], k[h][:half]) for h in heads]
    gram_bottom = [mm_nt(k[h][half:], k[h]) for h in heads]
    squares = [
        jnp.concatenate(
            [
                jnp.sum(jnp.where(eye_half, g, 0.0), axis=0, keepdims=True)
                for g in (gram_top[h], gram_bottom[h][:, half:])
            ],
            axis=1,
        )
        for h in heads
    ]
    k_row = lax.rsqrt(jnp.concatenate(squares, axis=0) + epsilon)
    k_col = k_row.T
    left = beta_col * k_col
    carried = left * jnp.where(doc_col == start_doc, jnp.exp2(gs_col), 0.0)
    closing = k_col * jnp.where(doc_col == last_doc, jnp.exp2(gs_col[keys - 1:] - gs_col), 0.0)
    one_top = eye_half.astype(f32)
    one_bottom = jnp.concatenate([jnp.zeros((half, half), f32), one_top], axis=1)
    top, bottom, right = [], [], []
    for h in heads:
        gr, gc = gs_row[h:h + 1], gs_col[:, h:h + 1]
        kr, lc = k_row[h:h + 1], left[:, h:h + 1]
        top.append(
            split(
                jnp.where(
                    top_mask,
                    gram_top[h] * jnp.exp2(gc[:half] - gr[:, :half]) * kr[:, :half] * lc[:half],
                    one_top,
                )
            )
        )
        bottom.append(
            split(
                jnp.where(
                    bottom_mask,
                    gram_bottom[h] * jnp.exp2(gc[half:] - gr) * kr * lc[half:],
                    one_bottom,
                )
            )
        )

    blocks = [(h, b) for h in heads for b in range(2)]
    part = {(h, b): top[h][0] if b == 0 else bottom[h][0][:, half:] for h, b in blocks}
    inv = {key: eye16 - part[key] * masks[0] for key in blocks}
    for stage, mask in enumerate(masks[1:]):
        cross = {key: mm(inv[key], part[key] * mask).astype(bf16) for key in blocks}
        square = {key: mm(cross[key], cross[key]).astype(bf16) for key in blocks}
        near = {key: inv[key] - mm(cross[key], inv[key]).astype(bf16) for key in blocks}
        inv = {
            key: (near[key].astype(f32) + mm(square[key], near[key])).astype(bf16)
            for key in blocks
        }
        if stage == 0:
            for h in heads:
                right.append(
                    jnp.concatenate(
                        [
                            k[h].astype(f32) * carried[:, h:h + 1],
                            v[h].astype(f32) * beta_col[:, h:h + 1],
                        ],
                        axis=1,
                    )
                )
        if stage == 1:
            probes, norms = [], []
            for h in heads:
                gr, gt = gs_row[h:h + 1], gs_tok[:, h:h + 1]
                q_norm = unit(q[h].astype(f32))
                norms.append(q_norm)
                probes.append(
                    jnp.where(
                        tok_linked, mm_nt(q[h], k[h]) * jnp.exp2(gt - gr) * k_row[h:h + 1] * q_norm, 0.0
                    )
                )
    lower = []
    for h in heads:
        inner = mm(bottom[h][0][:, :half], inv[h, 0]).astype(bf16)
        lower.append(
            jnp.concatenate([-mm(inv[h, 1], inner).astype(bf16), inv[h, 1]], axis=1)
        )

    both = []
    for h in heads:
        rough = right[h].astype(bf16)
        g_top = mm(inv[h, 0], rough[:half]).astype(bf16)
        g_bottom = mm(lower[h], rough).astype(bf16)
        rest_top = right[h][:half] - mm(
            jnp.concatenate(top[h], axis=1), jnp.concatenate([g_top, g_top], axis=0)
        )
        rest_bottom = right[h][half:] - mm(
            jnp.concatenate(bottom[h], axis=1),
            jnp.concatenate([g_top, g_bottom, g_top, g_bottom], axis=0),
        )
        rest_top, rest_bottom = rest_top.astype(bf16), rest_bottom.astype(bf16)
        both.append(
            jnp.concatenate(
                [
                    mm(
                        jnp.concatenate([inv[h, 0], eye16], axis=1),
                        jnp.concatenate([rest_top, g_top], axis=0),
                    ),
                    mm(
                        jnp.concatenate([lower[h], eye16], axis=1),
                        jnp.concatenate([rest_top, rest_bottom, g_bottom], axis=0),
                    ),
                ],
                axis=0,
            )
        )

    carried_tok = jnp.where(doc_tok == start_doc, jnp.exp2(gs_tok), 0.0)
    for h in heads:
        q32 = q[h].astype(f32)
        q_norm = norms[h]
        outs = dot3(probes[h], both[h])
        reach_ref[h] = (carried_tok[:, h:h + 1] * q_norm) * q32 - outs[:, :size]
        own_ref[h] = outs[:, size:]
    departures = [
        pltpu.make_async_copy(reach_ref, reach_hbm, sems.at[10]),
        pltpu.make_async_copy(own_ref, own_hbm, sems.at[11]),
    ]
    for copy in departures:
        copy.start()
    for h in heads:
        end_high, end_low = split(both[h] * closing[:, h:h + 1])
        ends = mm_tn(k[h], end_high) + mm_tn(k[h], end_low)
        keep = jnp.where(last_doc == start_doc, jnp.exp2(gs_row[h:h + 1, keys - 1:]), 0.0)
        transit_ref[h] = keep * eye_size - ends[:, :size]
        filled_ref[h] = ends[:, size:]
    for copy in departures + ahead_copies:
        copy.wait()


def local_terms(seq, offset, resets, arrays, loaded, earlier=()):
    count, tok, packed = arrays[0].shape
    head_count = arrays[3].shape[1]
    size = packed // head_count
    fetch, ahead = loaded is None, seq + 1 < count
    smem, hbm = pl.BlockSpec(memory_space=pltpu.SMEM), pl.BlockSpec(memory_space=pltpu.HBM)
    operands = list(arrays) if fetch else list(loaded) + (list(arrays) if ahead else [])
    specs = [hbm] * 5 if fetch else vmem(5) + ([hbm] * 5 if ahead else [])
    squares = [pltpu.VMEM((head_count, size, size), f32)] * 2
    talls = [pltpu.HBM((head_count, tok, size), f32)] * 2
    blocks = [pltpu.VMEM(x.shape[1:], x.dtype) for x in arrays]
    outs = pl.pallas_call(
        functools.partial(local_kernel, head_count, seq, fetch, ahead, len(earlier)),
        in_specs=[smem, smem] + specs + untouched(earlier),
        out_specs=vmem(2) + [hbm] * 2 + (vmem(5) if ahead else []),
        out_shape=squares + talls + (blocks if ahead else []),
        scratch_shapes=[pltpu.VMEM((head_count, tok, size), f32)] * 2
        + [pltpu.SemaphoreType.DMA((12,))]
        + (blocks if fetch else []),
        compiler_params=pltpu.CompilerParams(vmem_limit_bytes=16 << 20),
        name="local_terms",
    )(offset, resets, *operands, *earlier)
    return outs[:4], outs[4:]


def vmem(count):
    return [pl.BlockSpec(memory_space=pltpu.VMEM)] * count


def untouched(earlier):
    return [pl.BlockSpec(memory_space=pl.ANY)] * len(earlier)


def step_kernel(choices, here_ref, *refs):
    maps, fills, state_ref = refs[:choices], refs[choices:2 * choices], refs[2 * choices]
    out_ref, mark_ref = refs[-2:]
    mark_ref[...] = jnp.zeros_like(mark_ref)
    here = here_ref[0]
    for n in range(choices):

        @pl.when(here == n)
        def _(n=n):
            for h in range(state_ref.shape[0]):
                out_ref[h] = dot3(maps[n][h], state_ref[h]) + fills[n][h]

    @pl.when(jnp.logical_or(here < 0, here >= choices))
    def _():
        out_ref[...] = fills[0][...]


def step(here, maps, fills, state, earlier=()):
    return pl.pallas_call(
        functools.partial(step_kernel, len(maps)),
        in_specs=[pl.BlockSpec(memory_space=pltpu.SMEM)]
        + vmem(2 * len(maps) + 1)
        + untouched(earlier),
        out_specs=vmem(2),
        out_shape=[pltpu.VMEM(state.shape, f32), pltpu.VMEM((8, 128), f32)],
        compiler_params=pltpu.CompilerParams(vmem_limit_bytes=8 << 20),
        cost_estimate=small_cost,
        name="state_step",
    )(here, *maps, *fills, state, *earlier)


def project_kernel(choices, groups, here_ref, place_ref, reach_ref, own_ref, *refs):
    states, w_ref = refs[:choices], refs[choices]
    keep_ref, head_ref, state_ref = refs[-3:]
    send_refs = refs[-3 - groups // 2:-3]
    heads, _, size = reach_ref.shape
    here, place = here_ref[0], place_ref[0]
    part = w_ref.shape[1] // groups

    @pl.when(here == 0)
    def _():
        for h in range(heads):
            head_ref[:, h * size:(h + 1) * size] = own_ref[h].astype(bf16)

    @pl.when(here > 0)
    def _():
        for n in range(choices):

            @pl.when(here == n + 1)
            def _(n=n):
                state_ref[...] = states[n][...]

        for h in range(heads):
            mixed = own_ref[h] + dot3(reach_ref[h], state_ref[h])
            head_ref[:, h * size:(h + 1) * size] = mixed.astype(bf16)

    for r in range(groups):
        start = pl.multiple_of((place ^ r) * part, part)
        share = mm(head_ref[...], w_ref[:, pl.ds(start, part)])
        if r % 2:
            send_refs[r // 2][...] = share
        else:
            keep_ref[r // 2] = share


def project(groups, here, place, reach, own, states, w_out, earlier=()):
    heads, tok, size = reach.shape
    part = w_out.shape[1] // groups
    mid = groups // 2
    smem = pl.BlockSpec(memory_space=pltpu.SMEM)
    outs = pl.pallas_call(
        functools.partial(project_kernel, len(states), groups),
        in_specs=[smem, smem] + vmem(3 + len(states)) + untouched(earlier),
        out_specs=vmem(mid + 1),
        out_shape=[pltpu.VMEM((tok, part), f32)] * mid
        + [pltpu.VMEM((mid, tok, part), f32)],
        scratch_shapes=[
            pltpu.VMEM((tok, heads * size), bf16),
            pltpu.VMEM((heads, size, size), f32),
        ],
        compiler_params=pltpu.CompilerParams(vmem_limit_bytes=16 << 20),
        cost_estimate=small_cost,
        name="project",
    )(here, place, reach, own, *states, w_out, *earlier)
    return outs[:mid], outs[mid]


def swapped(x, axis, bit):
    size = lax.axis_size(axis)
    return lax.ppermute(x, axis, [(i, i ^ bit) for i in range(size)])


def carry_on(devices, x, round_index, chunks):
    pairs = [(i, i + 1) for i in range(devices - 1) if 0 <= round_index - i < chunks]
    return lax.ppermute(x, "seq", pairs)


def add_kernel(mine_ref, *refs):
    leave_ref, stay_ref = refs[-2:]
    for r in range(mine_ref.shape[0]):
        out_ref = leave_ref if r % 2 else stay_ref
        out_ref[r // 2] = mine_ref[r] + refs[r][...]


def add_parts(mine, others, earlier=()):
    part = pltpu.VMEM((mine.shape[0] // 2,) + mine.shape[1:], f32)
    return pl.pallas_call(
        add_kernel,
        in_specs=vmem(1 + len(others)) + untouched(earlier),
        out_specs=vmem(2),
        out_shape=[part] * 2,
        compiler_params=pltpu.CompilerParams(vmem_limit_bytes=4 << 20),
        cost_estimate=small_cost,
        name="add_parts",
    )(mine, *others, *earlier)


def reduced(send, keep):
    bit = 2
    while True:
        other = swapped(send, "head", bit)
        if keep.shape[0] == 1:
            return keep[0], other[0]
        send, keep = add_parts(keep, list(other))
        bit *= 2


def shards(queries, keys, values, log_gate, beta, resets, w_out):
    chunks, tok, packed = queries.shape
    groups = lax.axis_size("head")
    devices = lax.axis_size("seq")
    here = lax.axis_index("seq").astype(jnp.int32).reshape(1)
    offset = here * tok
    place = lax.axis_index("head").astype(jnp.int32).reshape(1)

    arrays = [
        pltpu.with_memory_space_constraint(x, pltpu.HBM)
        for x in (queries, keys, values, log_gate, beta)
    ]
    resets = pltpu.with_memory_space_constraint(resets, pltpu.HBM)
    loaded = None

    if devices > 8:
        terms = []
        for s in range(chunks):
            term, loaded = local_terms(s, offset, resets, arrays, loaded)
            terms.append(term)
        pairs = [(i, i + 1) for i in range(devices - 1)]
        no_choice = jnp.zeros((1,), jnp.int32)

        def turn(_, incoming):
            return tuple(
                lax.ppermute(
                    step(no_choice, [terms[s][0]], [terms[s][1]], incoming[s])[0], "seq", pairs
                )
                for s in range(chunks)
            )

        zero = tuple(jnp.zeros_like(terms[s][1]) for s in range(chunks))
        states = lax.fori_loop(0, devices - 1, turn, zero)
        outs = []
        for s in range(chunks):
            one = jnp.ones((1,), jnp.int32)
            sends, keep = project(groups, one, place, terms[s][2], terms[s][3], [states[s]], w_out)
            leave, stay = add_parts(keep, [swapped(x, "head", 1) for x in sends])
            outs.append(reduced(leave, stay))
        return jnp.stack([mine + other for mine, other in outs])

    last_round = chunks + devices - 3
    terms, arrived, partial, outs = [], [], [], []
    token = ()

    def add_up(c, token):
        sends, keep = partial[c]
        settled = (outs[c - 2][1],) if c == chunks - 1 and c >= 2 else ()
        leave, stay = add_parts(keep, [swapped(x, "head", 1) for x in sends], token + settled)
        outs.append(reduced(leave, stay))
        return (leave,)

    def projected(c, token):
        if 2 <= c < chunks - 1:
            token = token + (outs[c - 2][1],)
        partial.append(
            project(
                groups, here, place, terms[c][2], terms[c][3],
                [arrived[c + i] for i in range(devices - 1)], w_out, token,
            )
        )
        return (partial[c][1],)

    for r in range(last_round + 1):
        if r < chunks:
            term, loaded = local_terms(r, offset, resets, arrays, loaded, token)
            terms.append(term)
            token = (term[1],)
        if r == 0:
            sent = terms[0][1]
        else:
            valid = [r - i for i in range(devices - 1) if 0 <= r - i < chunks]
            sent, mark = step(
                here - (r - valid[0]),
                [terms[c][0] for c in valid],
                [terms[c][1] for c in valid],
                arrived[r - 1],
                token,
            )
            token = (mark,)
        arrived.append(carry_on(devices, sent, r, chunks))
        done = r - devices + 1
        if done >= 0:
            token = projected(done, token)
        if done >= 1:
            token = add_up(done - 1, token)
    done = last_round - devices + 2
    token = projected(done, token)
    token = add_up(done - 1, token)
    token = add_up(done, token)
    return jnp.stack([mine + other for mine, other in outs])


def solution(mesh):
    placed = (
        P("grp", "seq", "head"),
        P("grp", "seq", None, "head"),
        P("grp", "seq", None, "head"),
        P("grp", "head", "seq"),
        P("grp", None, "head", "seq"),
        P("grp", None),
        P("head", None),
    )
    return jax.shard_map(
        shards, mesh=mesh, in_specs=placed, out_specs=P("grp", "seq", "head"), check_vma=False
    )
```

```python
import functools

import jax
import jax.numpy as jnp
from jax import lax
from jax.experimental import pallas as pl
from jax.experimental.pallas import tpu as pltpu
from jax.sharding import PartitionSpec as P

epsilon = 1e-06
log2_e = 1.4426950408889634
small_cost = pl.CostEstimate(flops=1 << 20, transcendentals=0, bytes_accessed=1 << 10)
f32 = jnp.float32
bf16 = jnp.bfloat16


def mm(a, b):
    return lax.dot_general(a, b, (((1,), (0,)), ((), ())), preferred_element_type=f32)


def mm_nt(a, b):
    return lax.dot_general(a, b, (((1,), (1,)), ((), ())), preferred_element_type=f32)


def mm_tn(a, b):
    return lax.dot_general(a, b, (((0,), (0,)), ((), ())), preferred_element_type=f32)


def split(x):
    high = x.astype(bf16)
    return high, (x - high.astype(f32)).astype(bf16)


def split3(x):
    high, rest = x.astype(bf16), None
    rest = x - high.astype(f32)
    middle = rest.astype(bf16)
    return high, middle, (rest - middle.astype(f32)).astype(bf16)


def dot3(a, b):
    a_high, a_low = split(a)
    b_high, b_low = split(b)
    return mm(a_high, b_high) + (mm(a_low, b_high) + mm(a_high, b_low))


def iota(shape, axis):
    return lax.broadcasted_iota(jnp.int32, shape, axis)


def local_kernel(head_count, seq, fetch, ahead, later, offset_ref, resets_ref, *refs):
    refs = list(refs)
    inputs = [refs.pop(0) for _ in range(5)]
    sources = inputs if fetch else [refs.pop(0) for _ in range(5)] if ahead else []
    refs = refs[later:]
    transit_ref, filled_ref, reach_hbm, own_hbm = [refs.pop(0) for _ in range(4)]
    nexts = [refs.pop(0) for _ in range(5)] if ahead else []
    reach_ref, own_ref, sems = refs.pop(0), refs.pop(0), refs.pop(0)
    arrivals, ahead_copies = [], []
    if fetch:
        arrivals = [
            pltpu.make_async_copy(source.at[seq], refs[n], sems.at[n])
            for n, source in enumerate(sources)
        ]
        inputs = refs
    if ahead:
        ahead_copies = [
            pltpu.make_async_copy(source.at[seq + 1], nexts[n], sems.at[5 + n])
            for n, source in enumerate(sources)
        ]
    for copy in arrivals + ahead_copies:
        copy.start()
    q_ref, k_ref, v_ref, gate_ref, beta_ref = inputs
    tok = q_ref.shape[0]
    size = q_ref.shape[1] // head_count
    keys = 2 * tok
    half = keys // 2
    heads = range(head_count)
    offset = offset_ref[0]
    reset = [resets_ref[seq, i] for i in range(resets_ref.shape[1])]

    def doc_of(position):
        total = jnp.zeros_like(position)
        for r in reset:
            total = total + (r <= position).astype(jnp.int32)
        return total

    start_doc = sum(((r < offset).astype(jnp.int32) for r in reset), jnp.int32(0))
    last_doc = sum(((r <= offset + tok - 1).astype(jnp.int32) for r in reset), jnp.int32(0))
    doc_row = doc_of(offset + (iota((1, keys), 1) >> 1))
    doc_col = doc_of(offset + (iota((keys, 1), 0) >> 1))
    doc_tok = doc_of(offset + iota((tok, 1), 0))

    def stacked(x):
        return jnp.concatenate([p.astype(f32) for p in split3(x)], axis=0).astype(bf16)

    def folded(m):
        n = head_count
        return m[:n] + m[n:2 * n] + m[2 * n:3 * n]

    tok_i, key_i = iota((tok, keys), 0), iota((tok, keys), 1)
    for copy in arrivals:
        copy.wait()
    gate3 = stacked(gate_ref[...])
    gs_row = log2_e * folded(mm(gate3, (tok_i <= (key_i >> 1)).astype(f32).astype(bf16)))
    beta_row = folded(
        mm(stacked(beta_ref[0]), (key_i == 2 * tok_i).astype(f32).astype(bf16))
        + mm(stacked(beta_ref[1]), (key_i == 2 * tok_i + 1).astype(f32).astype(bf16))
    )
    gs_tok_row = log2_e * folded(
        mm(gate3, (iota((tok, tok), 0) <= iota((tok, tok), 1)).astype(f32).astype(bf16))
    )
    gs_col, beta_col, gs_tok = gs_row.T, beta_row.T, gs_tok_row.T

    h_i, h_j = iota((half, half), 0), iota((half, half), 1)
    eye_half = h_i == h_j
    apart = jnp.where(h_i > h_j, h_i ^ h_j, 0)
    spans = [(1, 2)]
    while spans[-1][1] < half:
        spans.append((spans[-1][1], min(4 * spans[-1][1], half)))
    masks = [
        jnp.logical_and(apart >= a, apart < b).astype(f32).astype(bf16) for a, b in spans
    ]
    eye16 = eye_half.astype(f32).astype(bf16)
    eye_size = (iota((size, size), 0) == iota((size, size), 1)).astype(f32)
    top_mask = jnp.logical_and(h_i > h_j, doc_col[:half] == doc_row[:, :half])
    low_i, low_j = iota((half, keys), 0), iota((half, keys), 1)
    bottom_mask = jnp.logical_and(low_i + half > low_j, doc_col[half:] == doc_row)
    tok_linked = jnp.logical_and(
        (iota((tok, keys), 1) >> 1) <= iota((tok, keys), 0), doc_tok == doc_row
    )

    q = [q_ref[:, h * size:(h + 1) * size] for h in heads]
    k = [k_ref[:, :, h * size:(h + 1) * size].astype(f32).reshape(2 * tok, size).astype(bf16) for h in heads]
    v = [v_ref[:, :, h * size:(h + 1) * size].astype(f32).reshape(2 * tok, size).astype(bf16) for h in heads]

    def unit(x):
        return lax.rsqrt(jnp.sum(x * x, axis=1, keepdims=True) + epsilon)

    gram_top = [mm_nt(k[h][:half], k[h][:half]) for h in heads]
    gram_bottom = [mm_nt(k[h][half:], k[h]) for h in heads]
    squares = [
        jnp.concatenate(
            [
                jnp.sum(jnp.where(eye_half, g, 0.0), axis=0, keepdims=True)
                for g in (gram_top[h], gram_bottom[h][:, half:])
            ],
            axis=1,
        )
        for h in heads
    ]
    k_row = lax.rsqrt(jnp.concatenate(squares, axis=0) + epsilon)
    k_col = k_row.T
    left = beta_col * k_col
    carried = left * jnp.where(doc_col == start_doc, jnp.exp2(gs_col), 0.0)
    closing = k_col * jnp.where(doc_col == last_doc, jnp.exp2(gs_col[keys - 1:] - gs_col), 0.0)
    one_top = eye_half.astype(f32)
    one_bottom = jnp.concatenate([jnp.zeros((half, half), f32), one_top], axis=1)
    top, bottom, right = [], [], []
    for h in heads:
        gr, gc = gs_row[h:h + 1], gs_col[:, h:h + 1]
        kr, lc = k_row[h:h + 1], left[:, h:h + 1]
        top.append(
            split(
                jnp.where(
                    top_mask,
                    gram_top[h] * jnp.exp2(gc[:half] - gr[:, :half]) * kr[:, :half] * lc[:half],
                    one_top,
                )
            )
        )
        bottom.append(
            split(
                jnp.where(
                    bottom_mask,
                    gram_bottom[h] * jnp.exp2(gc[half:] - gr) * kr * lc[half:],
                    one_bottom,
                )
            )
        )

    blocks = [(h, b) for h in heads for b in range(2)]
    part = {(h, b): top[h][0] if b == 0 else bottom[h][0][:, half:] for h, b in blocks}
    inv = {key: eye16 - part[key] * masks[0] for key in blocks}
    for stage, mask in enumerate(masks[1:]):
        cross = {key: mm(inv[key], part[key] * mask).astype(bf16) for key in blocks}
        square = {key: mm(cross[key], cross[key]).astype(bf16) for key in blocks}
        near = {key: inv[key] - mm(cross[key], inv[key]).astype(bf16) for key in blocks}
        inv = {
            key: (near[key].astype(f32) + mm(square[key], near[key])).astype(bf16)
            for key in blocks
        }
        if stage == 0:
            for h in heads:
                right.append(
                    jnp.concatenate(
                        [
                            k[h].astype(f32) * carried[:, h:h + 1],
                            v[h].astype(f32) * beta_col[:, h:h + 1],
                        ],
                        axis=1,
                    )
                )
        if stage == 1:
            probes, norms = [], []
            for h in heads:
                gr, gt = gs_row[h:h + 1], gs_tok[:, h:h + 1]
                q_norm = unit(q[h].astype(f32))
                norms.append(q_norm)
                probes.append(
                    jnp.where(
                        tok_linked, mm_nt(q[h], k[h]) * jnp.exp2(gt - gr) * k_row[h:h + 1] * q_norm, 0.0
                    )
                )
    lower = []
    for h in heads:
        inner = mm(bottom[h][0][:, :half], inv[h, 0]).astype(bf16)
        lower.append(
            jnp.concatenate([-mm(inv[h, 1], inner).astype(bf16), inv[h, 1]], axis=1)
        )

    both = []
    for h in heads:
        rough = right[h].astype(bf16)
        g_top = mm(inv[h, 0], rough[:half]).astype(bf16)
        g_bottom = mm(lower[h], rough).astype(bf16)
        rest_top = right[h][:half] - mm(
            jnp.concatenate(top[h], axis=1), jnp.concatenate([g_top, g_top], axis=0)
        )
        rest_bottom = right[h][half:] - mm(
            jnp.concatenate(bottom[h], axis=1),
            jnp.concatenate([g_top, g_bottom, g_top, g_bottom], axis=0),
        )
        rest_top, rest_bottom = rest_top.astype(bf16), rest_bottom.astype(bf16)
        both.append(
            jnp.concatenate(
                [
                    mm(
                        jnp.concatenate([inv[h, 0], eye16], axis=1),
                        jnp.concatenate([rest_top, g_top], axis=0),
                    ),
                    mm(
                        jnp.concatenate([lower[h], eye16], axis=1),
                        jnp.concatenate([rest_top, rest_bottom, g_bottom], axis=0),
                    ),
                ],
                axis=0,
            )
        )

    carried_tok = jnp.where(doc_tok == start_doc, jnp.exp2(gs_tok), 0.0)
    for h in heads:
        q32 = q[h].astype(f32)
        q_norm = norms[h]
        outs = dot3(probes[h], both[h])
        reach_ref[h] = (carried_tok[:, h:h + 1] * q_norm) * q32 - outs[:, :size]
        own_ref[h] = outs[:, size:]
    departures = [
        pltpu.make_async_copy(reach_ref, reach_hbm, sems.at[10]),
        pltpu.make_async_copy(own_ref, own_hbm, sems.at[11]),
    ]
    for copy in departures:
        copy.start()
    for h in heads:
        end_high, end_low = split(both[h] * closing[:, h:h + 1])
        ends = mm_tn(k[h], end_high) + mm_tn(k[h], end_low)
        keep = jnp.where(last_doc == start_doc, jnp.exp2(gs_row[h:h + 1, keys - 1:]), 0.0)
        transit_ref[h] = keep * eye_size - ends[:, :size]
        filled_ref[h] = ends[:, size:]
    for copy in departures + ahead_copies:
        copy.wait()


def local_terms(seq, offset, resets, arrays, loaded, earlier=()):
    count, tok, packed = arrays[0].shape
    head_count = arrays[3].shape[1]
    size = packed // head_count
    fetch, ahead = loaded is None, seq + 1 < count
    smem, hbm = pl.BlockSpec(memory_space=pltpu.SMEM), pl.BlockSpec(memory_space=pltpu.HBM)
    operands = list(arrays) if fetch else list(loaded) + (list(arrays) if ahead else [])
    specs = [hbm] * 5 if fetch else vmem(5) + ([hbm] * 5 if ahead else [])
    squares = [pltpu.VMEM((head_count, size, size), f32)] * 2
    talls = [pltpu.HBM((head_count, tok, size), f32)] * 2
    blocks = [pltpu.VMEM(x.shape[1:], x.dtype) for x in arrays]
    outs = pl.pallas_call(
        functools.partial(local_kernel, head_count, seq, fetch, ahead, len(earlier)),
        in_specs=[smem, smem] + specs + untouched(earlier),
        out_specs=vmem(2) + [hbm] * 2 + (vmem(5) if ahead else []),
        out_shape=squares + talls + (blocks if ahead else []),
        scratch_shapes=[pltpu.VMEM((head_count, tok, size), f32)] * 2
        + [pltpu.SemaphoreType.DMA((12,))]
        + (blocks if fetch else []),
        compiler_params=pltpu.CompilerParams(vmem_limit_bytes=16 << 20),
        name="local_terms",
    )(offset, resets, *operands, *earlier)
    return outs[:4], outs[4:]


def vmem(count):
    return [pl.BlockSpec(memory_space=pltpu.VMEM)] * count


def untouched(earlier):
    return [pl.BlockSpec(memory_space=pl.ANY)] * len(earlier)


def step_kernel(choices, here_ref, *refs):
    maps, fills, state_ref = refs[:choices], refs[choices:2 * choices], refs[2 * choices]
    out_ref, mark_ref = refs[-2:]
    mark_ref[...] = jnp.zeros_like(mark_ref)
    here = here_ref[0]
    for n in range(choices):

        @pl.when(here == n)
        def _(n=n):
            for h in range(state_ref.shape[0]):
                out_ref[h] = dot3(maps[n][h], state_ref[h]) + fills[n][h]

    @pl.when(jnp.logical_or(here < 0, here >= choices))
    def _():
        out_ref[...] = fills[0][...]


def step(here, maps, fills, state, earlier=()):
    return pl.pallas_call(
        functools.partial(step_kernel, len(maps)),
        in_specs=[pl.BlockSpec(memory_space=pltpu.SMEM)]
        + vmem(2 * len(maps) + 1)
        + untouched(earlier),
        out_specs=vmem(2),
        out_shape=[pltpu.VMEM(state.shape, f32), pltpu.VMEM((8, 128), f32)],
        compiler_params=pltpu.CompilerParams(vmem_limit_bytes=8 << 20),
        cost_estimate=small_cost,
        name="state_step",
    )(here, *maps, *fills, state, *earlier)


def project_kernel(choices, groups, here_ref, place_ref, reach_ref, own_ref, *refs):
    states, w_ref = refs[:choices], refs[choices]
    keep_ref, head_ref, state_ref = refs[-3:]
    send_refs = refs[-3 - groups // 2:-3]
    heads, _, size = reach_ref.shape
    here, place = here_ref[0], place_ref[0]
    part = w_ref.shape[1] // groups

    @pl.when(here == 0)
    def _():
        for h in range(heads):
            head_ref[:, h * size:(h + 1) * size] = own_ref[h].astype(bf16)

    @pl.when(here > 0)
    def _():
        for n in range(choices):

            @pl.when(here == n + 1)
            def _(n=n):
                state_ref[...] = states[n][...]

        for h in range(heads):
            mixed = own_ref[h] + dot3(reach_ref[h], state_ref[h])
            head_ref[:, h * size:(h + 1) * size] = mixed.astype(bf16)

    for r in range(groups):
        start = pl.multiple_of((place ^ r) * part, part)
        share = mm(head_ref[...], w_ref[:, pl.ds(start, part)])
        if r % 2:
            send_refs[r // 2][...] = share
        else:
            keep_ref[r // 2] = share


def project(groups, here, place, reach, own, states, w_out, earlier=()):
    heads, tok, size = reach.shape
    part = w_out.shape[1] // groups
    mid = groups // 2
    smem = pl.BlockSpec(memory_space=pltpu.SMEM)
    outs = pl.pallas_call(
        functools.partial(project_kernel, len(states), groups),
        in_specs=[smem, smem] + vmem(3 + len(states)) + untouched(earlier),
        out_specs=vmem(mid + 1),
        out_shape=[pltpu.VMEM((tok, part), f32)] * mid
        + [pltpu.VMEM((mid, tok, part), f32)],
        scratch_shapes=[
            pltpu.VMEM((tok, heads * size), bf16),
            pltpu.VMEM((heads, size, size), f32),
        ],
        compiler_params=pltpu.CompilerParams(vmem_limit_bytes=16 << 20),
        cost_estimate=small_cost,
        name="project",
    )(here, place, reach, own, *states, w_out, *earlier)
    return outs[:mid], outs[mid]


def finish_kernel(first, count, *refs):
    out_ref, sums_ref, sems = refs[-3:]
    copies = []
    for n in range(count):
        sums_ref[n] = refs[2 * n][...] + refs[2 * n + 1][...]
        copies.append(
            pltpu.make_async_copy(sums_ref.at[n], out_ref.at[first + n], sems.at[n])
        )
        copies[n].start()
    for copy in copies:
        copy.wait()


def finish(pairs, first, chunks, begun=None):
    count, shape = len(pairs), pairs[0][0].shape
    hbm = pl.BlockSpec(memory_space=pltpu.HBM)
    held = [] if begun is None else [begun]
    return pl.pallas_call(
        functools.partial(finish_kernel, first, count),
        in_specs=vmem(2 * count) + [hbm] * len(held),
        out_specs=hbm,
        out_shape=pltpu.HBM((chunks,) + shape, f32),
        scratch_shapes=[pltpu.VMEM((count,) + shape, f32), pltpu.SemaphoreType.DMA((count,))],
        input_output_aliases={2 * count: 0} if held else {},
        compiler_params=pltpu.CompilerParams(vmem_limit_bytes=4 << 20),
        cost_estimate=small_cost,
        name="finish",
    )(*[x for pair in pairs for x in pair], *held)


def swapped(x, axis, bit):
    size = lax.axis_size(axis)
    return lax.ppermute(x, axis, [(i, i ^ bit) for i in range(size)])


def carry_on(devices, x, round_index, chunks):
    pairs = [(i, i + 1) for i in range(devices - 1) if 0 <= round_index - i < chunks]
    return lax.ppermute(x, "seq", pairs)


def add_kernel(mine_ref, *refs):
    leave_ref, stay_ref = refs[-2:]
    for r in range(mine_ref.shape[0]):
        out_ref = leave_ref if r % 2 else stay_ref
        out_ref[r // 2] = mine_ref[r] + refs[r][...]


def add_parts(mine, others, earlier=()):
    part = pltpu.VMEM((mine.shape[0] // 2,) + mine.shape[1:], f32)
    return pl.pallas_call(
        add_kernel,
        in_specs=vmem(1 + len(others)) + untouched(earlier),
        out_specs=vmem(2),
        out_shape=[part] * 2,
        compiler_params=pltpu.CompilerParams(vmem_limit_bytes=4 << 20),
        cost_estimate=small_cost,
        name="add_parts",
    )(mine, *others, *earlier)


def reduced(send, keep):
    bit = 2
    while True:
        other = swapped(send, "head", bit)
        if keep.shape[0] == 1:
            return keep[0], other[0]
        send, keep = add_parts(keep, list(other))
        bit *= 2


def shards(queries, keys, values, log_gate, beta, resets, w_out):
    chunks, tok, packed = queries.shape
    groups = lax.axis_size("head")
    devices = lax.axis_size("seq")
    here = lax.axis_index("seq").astype(jnp.int32).reshape(1)
    offset = here * tok
    place = lax.axis_index("head").astype(jnp.int32).reshape(1)

    arrays = [
        pltpu.with_memory_space_constraint(x, pltpu.HBM)
        for x in (queries, keys, values, log_gate, beta)
    ]
    resets = pltpu.with_memory_space_constraint(resets, pltpu.HBM)
    loaded = None

    if devices > 8:
        terms = []
        for s in range(chunks):
            term, loaded = local_terms(s, offset, resets, arrays, loaded)
            terms.append(term)
        pairs = [(i, i + 1) for i in range(devices - 1)]
        no_choice = jnp.zeros((1,), jnp.int32)

        def turn(_, incoming):
            return tuple(
                lax.ppermute(
                    step(no_choice, [terms[s][0]], [terms[s][1]], incoming[s])[0], "seq", pairs
                )
                for s in range(chunks)
            )

        zero = tuple(jnp.zeros_like(terms[s][1]) for s in range(chunks))
        states = lax.fori_loop(0, devices - 1, turn, zero)
        outs = []
        for s in range(chunks):
            one = jnp.ones((1,), jnp.int32)
            sends, keep = project(groups, one, place, terms[s][2], terms[s][3], [states[s]], w_out)
            leave, stay = add_parts(keep, [swapped(x, "head", 1) for x in sends])
            outs.append(reduced(leave, stay))
        return jnp.stack([mine + other for mine, other in outs])

    last_round = chunks + devices - 3
    terms, arrived, partial, outs = [], [], [], []
    token = ()

    def add_up(c, token):
        sends, keep = partial[c]
        settled = (outs[c - 2][1],) if c == chunks - 1 and c >= 2 else ()
        leave, stay = add_parts(keep, [swapped(x, "head", 1) for x in sends], token + settled)
        outs.append(reduced(leave, stay))
        return (leave,)

    def projected(c, token):
        if 2 <= c < chunks - 1:
            token = token + (outs[c - 2][1],)
        partial.append(
            project(
                groups, here, place, terms[c][2], terms[c][3],
                [arrived[c + i] for i in range(devices - 1)], w_out, token,
            )
        )
        return (partial[c][1],)

    for r in range(last_round + 1):
        if r < chunks:
            term, loaded = local_terms(r, offset, resets, arrays, loaded, token)
            terms.append(term)
            token = (term[1],)
        if r == 0:
            sent = terms[0][1]
        else:
            valid = [r - i for i in range(devices - 1) if 0 <= r - i < chunks]
            sent, mark = step(
                here - (r - valid[0]),
                [terms[c][0] for c in valid],
                [terms[c][1] for c in valid],
                arrived[r - 1],
                token,
            )
            token = (mark,)
        arrived.append(carry_on(devices, sent, r, chunks))
        done = r - devices + 1
        if done >= 0:
            token = projected(done, token)
        if done >= 1:
            token = add_up(done - 1, token)
    done = last_round - devices + 2
    token = projected(done, token)
    token = add_up(done - 1, token)
    token = add_up(done, token)
    return finish(outs[-1:], chunks - 1, chunks, finish(outs[:-1], 0, chunks))


def solution(mesh):
    placed = (
        P("grp", "seq", "head"),
        P("grp", "seq", None, "head"),
        P("grp", "seq", None, "head"),
        P("grp", "head", "seq"),
        P("grp", None, "head", "seq"),
        P("grp", None),
        P("head", None),
    )
    return jax.shard_map(
        shards, mesh=mesh, in_specs=placed, out_specs=P("grp", "seq", "head"), check_vma=False
    )
```
